256 devices in a mesh: cg: 16 (over z, x_lo), vg: 16 (over x_hi, y, core).
Axes of the slice: x: 4 (x_hi: 2, x_lo: 2; x = x_hi * 2 + x_lo), y: 4, z: 8, core: 2. Of those that a mesh axis runs over, the one named last changes fastest.
Arguments:
- con_embed: float32 [262144, 128], P(('cg', 'vg')), may hold values from -6 to 6
- var_embed: float32 [262144, 128], P(('vg', 'cg')), may hold values from -6 to 6
- row_coef: float32 [262144], P(('cg', 'vg')), may hold values from 0.3 to 3
- col_coef: float32 [262144], P(('vg', 'cg')), may hold values from 0.3 to 3
- self_weight: float32 [128, 128], replicated, may hold values from -0.5 to 0.5
- msg_weight: float32 [128, 128], replicated, may hold values from -0.0234375 to 0.0234375
- timestep: int32 [1], replicated, may hold values from 0 to 999
- tile_rows: int32 [16, 16, 16], P('cg', 'vg'), may hold values from 0 to 31, as said below
- tile_cols: int32 [16, 16, 16], P('cg', 'vg'), may hold values from 0 to 31, as said below
- pattern: bfloat16 [16, 16, 16, 512, 512], P('cg', 'vg'), may hold values from -6 to 6
- cotangent: float32 [262144, 128], P(('cg', 'vg')), may hold values from -6 to 6
Outputs:
- con_update: float32 [262144, 128], P(('cg', 'vg'))
- grad_con: float32 [262144, 128], P(('cg', 'vg'))
- grad_var: float32 [262144, 128], P(('vg', 'cg'))
- grad_msg: float32 [128, 128], replicated
- grad_self: float32 [128, 128], replicated
The draws below stay inside these ranges and needn't reach their ends.
Inputs may be any that keep to these rules, and one draw needn't show every extreme that they name: `tile_rows`: every device lists tile row 0 and tile row 31; a device lists distinct tiles unless 16 exceeds 32 * 32, and repeated tiles add. `tile_cols`: every device lists tile column 0 and tile column 31, together with the rows above: tiles (0, 0) and (31, 31) are on every list.
All inputs are finite; a program needn't handle non-finite values.
Results may differ from the reference program's by a relative error of at most 0.007.
Values may be sent and summed in bfloat16 or wider, within the bound.
No kernel may reach another device: no remote copies, remote signals or barrier semaphores. Data moves between devices by JAX's collectives and lax.ppermute only.
A program may use at most 128 MiB of HBM per device.

```python
import math
import jax
import jax.numpy as jnp
from jax import lax

H = 128
TB = 512
C_DEV = 1024
V_DEV = 1024
TILES = 16
NC = 262144
NV = 262144
RBLK = 32
CBLK = 32
N_CG = 16
N_VG = 16


def tile_pairs(key):
    block_total = RBLK * CBLK

    def single(subkey):
        perm_key, roll_key = jax.random.split(subkey)
        middle = jax.random.permutation(perm_key, block_total - 2) + 1
        listing = jnp.concatenate([jnp.array([block_total - 1, 0], dtype=jnp.int32), middle.astype(jnp.int32)])
        chosen = listing[jnp.arange(TILES, dtype=jnp.int32) % block_total]
        offset = jax.random.randint(roll_key, (), 0, TILES)
        return jnp.roll(chosen, offset)
    subkeys = jax.random.split(jax.random.fold_in(key, 11), N_CG * N_VG)
    chosen = jax.vmap(single)(subkeys).reshape(N_CG, N_VG, TILES)
    return (chosen // CBLK, chosen % CBLK)


def draw_tile_rows(key, part):
    return tile_pairs(key)[0]


def draw_tile_cols(key, part):
    return tile_pairs(key)[1]


def steps_of(stream_key, shape, pieces, low, high):
    def one(axis_at, blocks):
        heights = jax.random.uniform(jax.random.fold_in(jax.random.fold_in(stream_key, 6), axis_at), (blocks,), jnp.float32, low / len(pieces), high / len(pieces))
        return jnp.repeat(jnp.exp(heights), shape[axis_at] // blocks).reshape((-1,) + (1,) * (len(shape) - axis_at - 1))

    level = one(*pieces[0])
    for cut in pieces[1:]:
        level = level * one(*cut)
    return level


def gaussian(key, dims, width, most, cuts=(), kind=jnp.bfloat16):
    values = jax.random.normal(key, dims, jnp.float32) * width
    if len(cuts) > 0:
        values = steps_of(key, dims, cuts, -0.22, 0.18) * values
    return jnp.clip(values, min=-most, max=most).astype(kind)


def setup_inputs(seed: int = 0) -> dict:
    key_of = jax.random.split(jax.random.key(seed), 12)
    con_embed = gaussian(key_of[0], (NC, H), 1.0, 6.0, ((0, 256),), jnp.float32)
    var_embed = gaussian(key_of[1], (NV, H), 1.0, 6.0, ((0, 256),), jnp.float32)
    row_coef = jnp.clip(jnp.exp(math.log(3.0) - 2.3025851 * jax.random.uniform(key_of[2], (NC,), jnp.float32) ** steps_of(key_of[2], (NC,), ((0, 256),), -0.2, 0.2)), 0.3, 3.0)
    col_coef = jnp.clip(jnp.exp(math.log(3.0) - 2.3025851 * jax.random.uniform(key_of[3], (NV,), jnp.float32) ** steps_of(key_of[3], (NV,), ((0, 256),), -0.2, 0.2)), 0.3, 3.0)
    self_weight = gaussian(key_of[4], (H, H), H ** -0.5, 0.5, (), jnp.float32)
    msg_weight = gaussian(key_of[5], (H, H), (H * TB) ** -0.5, 0.0234375, (), jnp.float32)
    timestep = jax.random.randint(key_of[6], (1,), 0, 1000).astype(jnp.int32)
    tile_rows = draw_tile_rows(jax.random.fold_in(key_of[11], 71), 0)
    tile_cols = draw_tile_cols(jax.random.fold_in(key_of[11], 71), 0)
    pattern = gaussian(key_of[9], (N_CG, N_VG, TILES, TB, TB), 1.0, 6.0, ((0, 16), (1, 16)))
    cotangent = gaussian(key_of[10], (NC, H), 1.0, 6.0, ((0, 256),), jnp.float32)
    return dict(con_embed=con_embed, var_embed=var_embed, row_coef=row_coef, col_coef=col_coef, self_weight=self_weight, msg_weight=msg_weight, timestep=timestep, tile_rows=tile_rows, tile_cols=tile_cols, pattern=pattern, cotangent=cotangent)


def reference(con_embed, var_embed, row_coef, col_coef, self_weight, msg_weight, timestep, tile_rows, tile_cols, pattern, cotangent):
    highest = lax.Precision.HIGHEST
    group_rows = C_DEV * N_VG
    group_cols = V_DEV * N_CG
    row_list = tile_rows.reshape(-1, TILES)
    col_list = tile_cols.reshape(-1, TILES)
    pattern_list = pattern.reshape(-1, TILES, TB, TB)
    devices = jnp.arange(N_CG * N_VG, dtype=jnp.int32)
    projected = (jnp.dot(var_embed, msg_weight, precision=highest, preferred_element_type=jnp.float32) * col_coef[:, None]).astype(jnp.bfloat16)

    def forward(running, device):
        con_group = device // N_VG
        var_group = device % N_VG
        source = lax.dynamic_slice_in_dim(projected, (var_group * group_cols).astype(jnp.int32), group_cols, 0)
        source = source.reshape(CBLK, TB, H).astype(jnp.float32)
        tile_mask = pattern_list[device].astype(jnp.float32)
        products = jnp.einsum('trc,tch->trh', tile_mask, source[col_list[device]], precision=highest)
        selector = (row_list[device][None, :] == jnp.arange(RBLK, dtype=jnp.int32)[:, None]).astype(jnp.float32)
        partial_value = jnp.einsum('bt,trh->brh', selector, products, precision=highest).reshape(group_rows, H)
        offset = (con_group * group_rows).astype(jnp.int32)
        current = lax.dynamic_slice_in_dim(running, offset, group_rows, 0)
        return lax.dynamic_update_slice_in_dim(running, current + partial_value, offset, 0), None

    messages, _ = lax.scan(forward, jnp.zeros((NC, H), jnp.float32), devices)
    frequency = jnp.exp(-math.log(10000.0) * jnp.arange(H // 2, dtype=jnp.float32) / (H // 2))
    phases = timestep[0].astype(jnp.float32) * frequency
    time_embed = jnp.concatenate([jnp.sin(phases), jnp.cos(phases)])
    preact = jnp.dot(con_embed, self_weight, precision=highest, preferred_element_type=jnp.float32) + row_coef[:, None] * messages + time_embed[None, :]
    sigmoid_z = jax.nn.sigmoid(preact)
    con_update = con_embed + preact * sigmoid_z
    grad_pre = cotangent * sigmoid_z * (1.0 + preact * (1.0 - sigmoid_z))
    grad_con = cotangent + jnp.dot(grad_pre, self_weight.T, precision=highest, preferred_element_type=jnp.float32)
    grad_self = jnp.dot(con_embed.T, grad_pre, precision=highest, preferred_element_type=jnp.float32)
    grad_messages = (row_coef[:, None] * grad_pre).astype(jnp.bfloat16)

    def backward(running, device):
        con_group = device // N_VG
        var_group = device % N_VG
        source = lax.dynamic_slice_in_dim(grad_messages, (con_group * group_rows).astype(jnp.int32), group_rows, 0)
        source = source.reshape(RBLK, TB, H).astype(jnp.float32)
        tile_mask = pattern_list[device].astype(jnp.float32)
        products = jnp.einsum('trc,trh->tch', tile_mask, source[row_list[device]], precision=highest)
        selector = (col_list[device][None, :] == jnp.arange(CBLK, dtype=jnp.int32)[:, None]).astype(jnp.float32)
        partial_value = jnp.einsum('bt,tch->bch', selector, products, precision=highest).reshape(group_cols, H)
        offset = (var_group * group_cols).astype(jnp.int32)
        current = lax.dynamic_slice_in_dim(running, offset, group_cols, 0)
        return lax.dynamic_update_slice_in_dim(running, current + partial_value, offset, 0), None

    grad_projected, _ = lax.scan(backward, jnp.zeros((NV, H), jnp.float32), devices)
    grad_lin = col_coef[:, None] * grad_projected
    grad_var = jnp.dot(grad_lin, msg_weight.T, precision=highest, preferred_element_type=jnp.float32)
    grad_msg = jnp.dot(var_embed.T, grad_lin, precision=highest, preferred_element_type=jnp.float32)
    return (con_update, grad_con, grad_var, grad_msg, grad_self)
```

```python
import functools
import math

import jax
import jax.numpy as jnp
import numpy as np
from jax import lax
from jax.experimental import pallas as pl
from jax.experimental.pallas import tpu as pltpu
from jax.sharding import Mesh
from jax.sharding import PartitionSpec as P

H = 128
TB = 512
AXES = {"z": 8, "xl": 2, "xh": 2, "y": 4, "c": 2}
BF16 = jnp.bfloat16
F32 = jnp.float32


def shift(x, axis, by):
    n = AXES[axis]
    return lax.ppermute(x, axis, [(i, (i + by) % n) for i in range(n)])


def swap(x, axis, mask):
    return lax.ppermute(x, axis, [(i, i ^ mask) for i in range(AXES[axis])])


def ring_gather(x):
    half = x.shape[0] // 2
    parts = [(0, x)]
    up = down = x
    for step in (1, 2, 3):
        up, down = shift(up, "z", 1), shift(down, "z", -1)
        parts += [(2 * (8 - step), up), (2 * step, down)]
    parts += [(8, shift(up[:half], "z", 1)), (9, shift(down[half:], "z", -1))]
    return parts


def ring_scatter(sums):
    half = sums.shape[1] // 2
    up = shift(sums[4, :half].astype(BF16), "z", 1)
    down = shift(sums[4, half:].astype(BF16), "z", -1)
    up = jnp.concatenate([sums[3, :half] + up, sums[3, half:]]).astype(BF16)
    down = jnp.concatenate([sums[5, :half], sums[5, half:] + down]).astype(BF16)
    for step in (2, 1, 0):
        up, down = shift(up, "z", 1), shift(down, "z", -1)
        if step:
            up = (sums[step] + up).astype(BF16)
            down = (sums[8 - step] + down).astype(BF16)
    return sums[0] + up.astype(F32) + down.astype(F32)


def sum_all(x):
    for axis, masks in (("c", (1,)), ("xl", (1,)), ("xh", (1,)), ("y", (1, 2)), ("z", (1, 2, 4))):
        for mask in masks:
            x = x + swap(x, axis, mask)
    return x


def tile_kernel(places, transpose, take, put, *refs):
    n = len(places)
    sources, tiles, out = refs[:n], refs[n], refs[n + 1]
    source, held, total, source_sem, tile_sem, out_sem = refs[n + 2 :]
    count = held.shape[0]
    copies = [
        pltpu.make_async_copy(
            ref, source.at[pl.ds(place * TB, ref.shape[0])], source_sem.at[i]
        )
        for i, (place, ref) in enumerate(zip(places, sources, strict=True))
    ]
    for copy in copies:
        copy.start()

    def fetch(k):
        return pltpu.make_async_copy(tiles.at[k], held.at[k], tile_sem.at[k])

    for k in range(count):
        fetch(k).start()
    total[...] = jnp.zeros_like(total)
    for copy in copies:
        copy.wait()

    def step(k, carry):
        fetch(k).wait()
        begin = pl.multiple_of(take[k] * TB, TB)
        rows = source[pl.ds(begin, TB), :]
        target = pl.multiple_of(put[k] * TB, TB)
        for part in range(2):
            width = TB // 2
            cut = pl.ds(part * width, width)
            if transpose:
                product = lax.dot_general(
                    held[k, :, cut], rows, (((0,), (0,)), ((), ())), preferred_element_type=F32
                )
            else:
                product = jnp.dot(held[k, cut, :], rows, preferred_element_type=F32)
            at = pl.ds(pl.multiple_of(target + part * width, width), width)
            total[at, :] += product
        return carry

    lax.fori_loop(0, count, step, 0)
    copy = pltpu.make_async_copy(total, out, out_sem)
    copy.start()
    copy.wait()


def tile_products(parts, take, put, tiles, blocks, transpose):
    count = tiles.shape[0]
    arrays = [array for _, array in parts]
    flops = 2 * count * TB * TB * H
    return pl.pallas_call(
        functools.partial(tile_kernel, tuple(place for place, _ in parts), transpose),
        out_shape=jax.ShapeDtypeStruct((blocks * TB, H), F32),
        grid_spec=pltpu.PrefetchScalarGridSpec(
            num_scalar_prefetch=2,
            grid=(),
            in_specs=[pl.BlockSpec(memory_space=pl.ANY)] * (len(arrays) + 1),
            out_specs=pl.BlockSpec(memory_space=pl.ANY),
            scratch_shapes=[
                pltpu.VMEM((blocks * TB, H), BF16),
                pltpu.VMEM((count, TB, TB), BF16),
                pltpu.VMEM((blocks * TB, H), F32),
                pltpu.SemaphoreType.DMA((len(arrays),)),
                pltpu.SemaphoreType.DMA((count,)),
                pltpu.SemaphoreType.DMA,
            ],
        ),
        compiler_params=pltpu.CompilerParams(vmem_limit_bytes=28 << 20),
        cost_estimate=pl.CostEstimate(
            flops=flops, bytes_accessed=count * TB * TB * 2 + blocks * TB * H * 6, transcendentals=0
        ),
        name="tiles_back" if transpose else "tiles_forward",
    )(take, put, *arrays, tiles)


def body(
    con_embed,
    var_embed,
    row_coef,
    col_coef,
    self_weight,
    msg_weight,
    timestep,
    tile_rows,
    tile_cols,
    pattern,
    cotangent,
):
    dot = functools.partial(
        jnp.dot, precision=lax.Precision.HIGHEST, preferred_element_type=F32
    )
    rows_here = con_embed.shape[0]
    z, xl, core = lax.axis_index("z"), lax.axis_index("xl"), lax.axis_index("c")
    tiles = pattern.reshape(-1, TB, TB)
    row, col = tile_rows.reshape(-1), tile_cols.reshape(-1)
    row_owner, col_owner = row // 2, col // 2
    row_at = (((row_owner % 2) ^ core) * 8 + row_owner // 2) * 2 + row % 2
    col_at = (((col_owner % 2) ^ xl) * 8 + (col_owner // 2 - z) % 8) * 2 + col % 2

    projected = (dot(var_embed, msg_weight) * col_coef[:, None]).astype(BF16)
    near = ring_gather(projected)
    far = ring_gather(swap(projected, "xl", 1))
    parts = near + [(16 + place, array) for place, array in far]
    forward = tile_products(parts, col_at, row_at, tiles, 32, False)
    forward = forward.reshape(2, 8, rows_here, H)
    sibling = swap(forward[1].astype(BF16), "c", 1)
    partial = (forward[0] + sibling.astype(F32)).astype(BF16)
    partial = lax.all_to_all(partial, ("xh", "y"), split_axis=0, concat_axis=0, tiled=True)
    messages = jnp.sum(partial.astype(F32), axis=0)

    frequency = jnp.exp(-math.log(10000.0) * jnp.arange(H // 2, dtype=F32) / (H // 2))
    phases = timestep[0].astype(F32) * frequency
    time_embed = jnp.concatenate([jnp.sin(phases), jnp.cos(phases)])
    preact = dot(con_embed, self_weight) + row_coef[:, None] * messages + time_embed[None, :]
    sigmoid_z = jax.nn.sigmoid(preact)
    con_update = con_embed + preact * sigmoid_z
    grad_pre = cotangent * sigmoid_z * (1.0 + preact * (1.0 - sigmoid_z))
    grad_messages = (row_coef[:, None] * grad_pre).astype(BF16)

    copies = jnp.broadcast_to(grad_messages[None], (8, rows_here, H))
    own = lax.all_to_all(copies, ("xh", "y"), split_axis=0, concat_axis=0, tiled=True)
    own = own.reshape(8 * rows_here, H)
    other = swap(own, "c", 1)
    grad_con = cotangent + dot(grad_pre, self_weight.T)
    grad_self = sum_all(dot(con_embed.T, grad_pre))
    backward = tile_products([(0, own), (16, other)], row_at, col_at, tiles, 32, True)
    backward = backward.reshape(2, 8, rows_here, H)
    away = swap(ring_scatter(backward[1]).astype(BF16), "xl", 1)
    grad_projected = ring_scatter(backward[0]) + away.astype(F32)
    grad_lin = col_coef[:, None] * grad_projected
    grad_var = dot(grad_lin, msg_weight.T)
    grad_msg = sum_all(dot(var_embed.T, grad_lin))
    return (con_update, grad_con, grad_var, grad_msg, grad_self)


def solution(mesh):
    fine = Mesh(np.asarray(mesh.devices).reshape(tuple(AXES.values())), tuple(AXES))
    cg, vg = ("z", "xl"), ("xh", "y", "c")
    in_specs = (
        P(cg + vg, None),
        P(vg + cg, None),
        P(cg + vg),
        P(vg + cg),
        P(),
        P(),
        P(),
        P(cg, vg, None),
        P(cg, vg, None),
        P(cg, vg, None, None, None),
        P(cg + vg, None),
    )
    out_specs = (P(cg + vg, None), P(cg + vg, None), P(vg + cg, None), P(), P())
    return jax.shard_map(body, mesh=fine, in_specs=in_specs, out_specs=out_specs, check_vma=False)
```

```python
import functools
import math

import jax
import jax.numpy as jnp
import numpy as np
from jax import lax
from jax.experimental import pallas as pl
from jax.experimental.pallas import tpu as pltpu
from jax.sharding import Mesh
from jax.sharding import PartitionSpec as P

H = 128
TB = 512
AXES = {"z": 8, "xl": 2, "xh": 2, "y": 4, "c": 2}
BF16 = jnp.bfloat16
F32 = jnp.float32


def shift(x, axis, by):
    n = AXES[axis]
    return lax.ppermute(x, axis, [(i, (i + by) % n) for i in range(n)])


def swap(x, axis, mask):
    return lax.ppermute(x, axis, [(i, i ^ mask) for i in range(AXES[axis])])


def ring_gather(x):
    half = x.shape[0] // 2
    parts = [(0, x)]
    up = down = x
    for step in (1, 2, 3):
        up, down = shift(up, "z", 1), shift(down, "z", -1)
        parts += [(2 * (8 - step), up), (2 * step, down)]
    parts += [(8, shift(up[:half], "z", 1)), (9, shift(down[half:], "z", -1))]
    return parts


def ring_scatter(sums, first):
    half = sums.shape[1] // 2
    up = shift(first[:half], "z", 1)
    down = shift(first[half:], "z", -1)
    up = (sums[3] + jnp.pad(up.astype(F32), ((0, half), (0, 0)))).astype(BF16)
    down = (sums[5] + jnp.pad(down.astype(F32), ((half, 0), (0, 0)))).astype(BF16)
    for step in (2, 1, 0):
        up, down = shift(up, "z", 1), shift(down, "z", -1)
        if step:
            up = (sums[step] + up).astype(BF16)
            down = (sums[8 - step] + down).astype(BF16)
    return sums[0] + up.astype(F32) + down.astype(F32)


def sum_all(x):
    for axis, masks in (("c", (1,)), ("xl", (1,)), ("xh", (1,)), ("y", (1, 2)), ("z", (1, 2, 4))):
        for mask in masks:
            x = x + swap(x, axis, mask)
    return x


GRANT = 57 << 20
ANY_SPEC = pl.BlockSpec(memory_space=pl.ANY)
VMEM_SPEC = pl.BlockSpec(memory_space=pltpu.VMEM)


def each_tile(put, base, blocks, action):
    def step(k, carry):
        place = put[k] - base

        @pl.when((place >= 0) & (place < blocks))
        def _():
            action(k, place)

        return carry

    lax.fori_loop(0, put.shape[0], step, 0)


def add_products(take, put, copies, source, tiles, held, tile_sem, total, base, transpose):
    blocks = total.shape[0] // TB

    def fetch(k):
        return pltpu.make_async_copy(tiles.at[k], held.at[k], tile_sem.at[k])

    for copy in copies:
        copy.start()
    each_tile(put, base, blocks, lambda k, place: fetch(k).start())

    def clear(k, carry):
        total[pl.ds(pl.multiple_of(k * TB, TB), TB), :] = jnp.zeros((TB, H), F32)
        return carry

    lax.fori_loop(0, blocks, clear, 0)
    for copy in copies:
        copy.wait()

    def multiply(k, place):
        fetch(k).wait()
        rows = source[pl.ds(pl.multiple_of(take[k] * TB, TB), TB), :]
        width = TB // 2
        for part in range(2):
            cut = pl.ds(part * width, width)
            if transpose:
                product = lax.dot_general(
                    held[k, :, cut], rows, (((0,), (0,)), ((), ())), preferred_element_type=F32
                )
            else:
                product = jnp.dot(held[k, cut, :], rows, preferred_element_type=F32)
            at = pl.ds(pl.multiple_of(place * TB + part * width, width), width)
            total[at, :] += product

    each_tile(put, base, blocks, multiply)


def forward_kernel(places, base, take, put, *refs):
    n = len(places)
    sources, (tiles, out, source, held, total, source_sem, tile_sem) = refs[:n], refs[n:]
    copies = [
        pltpu.make_async_copy(
            ref, source.at[pl.ds(place * TB, ref.shape[0])], source_sem.at[i]
        )
        for i, (place, ref) in enumerate(zip(places, sources, strict=True))
    ]
    add_products(take, put, copies, source, tiles, held, tile_sem, total, base, False)

    def store(k, carry):
        at = pl.ds(pl.multiple_of(k * TB, TB), TB)
        out[at, :] = total[at, :].astype(out.dtype)
        return carry

    lax.fori_loop(0, out.shape[0] // TB, store, 0)


def tiles_forward(parts, take, put, tiles, base, dtype):
    arrays = [array for _, array in parts]
    count = tiles.shape[0]
    return pl.pallas_call(
        functools.partial(forward_kernel, tuple(place for place, _ in parts), base),
        out_shape=jax.ShapeDtypeStruct((16 * TB, H), dtype),
        grid_spec=pltpu.PrefetchScalarGridSpec(
            num_scalar_prefetch=2,
            grid=(),
            in_specs=[ANY_SPEC] * (len(arrays) + 1),
            out_specs=VMEM_SPEC,
            scratch_shapes=[
                pltpu.VMEM((32 * TB, H), BF16),
                pltpu.VMEM((count, TB, TB), BF16),
                pltpu.VMEM((16 * TB, H), F32),
                pltpu.SemaphoreType.DMA((len(arrays),)),
                pltpu.SemaphoreType.DMA((count,)),
            ],
        ),
        compiler_params=pltpu.CompilerParams(vmem_limit_bytes=GRANT),
        cost_estimate=pl.CostEstimate(
            flops=tiles.size * H, bytes_accessed=tiles.size + 32 * TB * H * 4, transcendentals=0
        ),
        name="tiles_forward",
    )(take, put, *arrays, tiles)


def back_kernel(
    z, take, put, own, other, tiles, scaled, sums, first, weight, source, held, total, right, sems, tile_sem
):
    half = own.shape[0]
    ins = [
        pltpu.make_async_copy(own, source.at[pl.ds(0, half)], sems.at[0]),
        pltpu.make_async_copy(other, source.at[pl.ds(half, half)], sems.at[1]),
    ]
    load = pltpu.make_async_copy(scaled, right, sems.at[2])
    load.start()
    add_products(take, put, ins, source, tiles, held, tile_sem, total, 0, True)
    out = pltpu.make_async_copy(total, sums, sems.at[3])
    out.start()
    rows = first.shape[1]
    for side in range(2):
        first[side] = total[pl.ds((side * 8 + 4) * rows, rows), :].astype(BF16)
    load.wait()
    weight[...] = jnp.zeros_like(weight)

    def contract(k, carry):
        side, place = k // 8, k % 8
        left = right[((z[0] + place) % 8) * 2 + side]
        block = total[pl.ds(pl.multiple_of(k * rows, rows), rows), :]
        high = block.astype(BF16)
        low = (block - high.astype(F32)).astype(BF16)
        for part in (high, low):
            weight[...] += lax.dot_general(
                left, part, (((0,), (0,)), ((), ())), preferred_element_type=F32
            )
        return carry

    lax.fori_loop(0, 16, contract, 0)
    out.wait()


def tiles_back(z, own, other, take, put, tiles, scaled):
    rows, count = scaled.shape[2], tiles.shape[0]
    scaled = scaled.reshape(16, rows, H)
    return pl.pallas_call(
        back_kernel,
        out_shape=(
            jax.ShapeDtypeStruct((16 * rows, H), F32),
            jax.ShapeDtypeStruct((2, rows, H), BF16),
            jax.ShapeDtypeStruct((H, H), F32),
        ),
        grid_spec=pltpu.PrefetchScalarGridSpec(
            num_scalar_prefetch=3,
            grid=(),
            in_specs=[ANY_SPEC] * 4,
            out_specs=(ANY_SPEC, VMEM_SPEC, VMEM_SPEC),
            scratch_shapes=[
                pltpu.VMEM((16 * rows, H), BF16),
                pltpu.VMEM((count, TB, TB), BF16),
                pltpu.VMEM((16 * rows, H), F32),
                pltpu.VMEM((16, rows, H), BF16),
                pltpu.SemaphoreType.DMA((4,)),
                pltpu.SemaphoreType.DMA((count,)),
            ],
        ),
        compiler_params=pltpu.CompilerParams(vmem_limit_bytes=GRANT),
        cost_estimate=pl.CostEstimate(
            flops=2 * tiles.size * H, bytes_accessed=2 * tiles.size + 32 * TB * H * 8, transcendentals=0
        ),
        name="tiles_back",
    )(z.reshape(1), take, put, own, other, tiles, scaled)


def body(
    con_embed,
    var_embed,
    row_coef,
    col_coef,
    self_weight,
    msg_weight,
    timestep,
    tile_rows,
    tile_cols,
    pattern,
    cotangent,
):
    dot = functools.partial(
        jnp.dot, precision=lax.Precision.HIGHEST, preferred_element_type=F32
    )
    rows_here = con_embed.shape[0]
    z, xl, core = lax.axis_index("z"), lax.axis_index("xl"), lax.axis_index("c")
    tiles = pattern.reshape(-1, TB, TB)
    row, col = tile_rows.reshape(-1), tile_cols.reshape(-1)
    row_owner, col_owner = row // 2, col // 2
    row_at = (((row_owner % 2) ^ core) * 8 + row_owner // 2) * 2 + row % 2
    col_at = (((col_owner % 2) ^ xl) * 8 + (col_owner // 2 - z) % 8) * 2 + col % 2

    projected = (dot(var_embed, msg_weight) * col_coef[:, None]).astype(BF16)
    near = ring_gather(projected)
    far = ring_gather(swap(projected, "xl", 1))
    parts = near + [(16 + place, array) for place, array in far]
    sibling = tiles_forward(parts, col_at, row_at, tiles, 16, BF16)
    scaled = (var_embed * col_coef[:, None]).astype(BF16)
    scaled = jnp.stack([scaled, swap(scaled, "xl", 1)])
    sibling, scaled = lax.optimization_barrier((sibling, scaled))
    scaled = lax.all_gather(scaled, "z", axis=0)
    sibling = swap(sibling, "c", 1)
    partial = tiles_forward(parts, col_at, row_at, tiles, 0, F32)
    partial = (partial + sibling.astype(F32)).astype(BF16)
    partial = partial.reshape(8, rows_here, H)
    partial = lax.all_to_all(partial, ("xh", "y"), split_axis=0, concat_axis=0, tiled=True)
    messages = jnp.sum(partial.astype(F32), axis=0)

    frequency = jnp.exp(-math.log(10000.0) * jnp.arange(H // 2, dtype=F32) / (H // 2))
    phases = timestep[0].astype(F32) * frequency
    time_embed = jnp.concatenate([jnp.sin(phases), jnp.cos(phases)])
    preact = dot(con_embed, self_weight) + row_coef[:, None] * messages + time_embed[None, :]
    sigmoid_z = jax.nn.sigmoid(preact)
    con_update = con_embed + preact * sigmoid_z
    grad_pre = cotangent * sigmoid_z * (1.0 + preact * (1.0 - sigmoid_z))
    grad_messages = (row_coef[:, None] * grad_pre).astype(BF16)

    copies = jnp.broadcast_to(grad_messages[None], (8, rows_here, H))
    own = lax.all_to_all(copies, ("xh", "y"), split_axis=0, concat_axis=0, tiled=True)
    own = own.reshape(8 * rows_here, H)
    other = swap(own, "c", 1)
    grad_con = cotangent + dot(grad_pre, self_weight.T)
    local_self = dot(con_embed.T, grad_pre)
    backward, first, local_msg = tiles_back(z, own, other, row_at, col_at, tiles, scaled)
    backward = backward.reshape(2, 8, rows_here, H)
    weights = sum_all(jnp.stack([local_self, local_msg]))
    away = swap(ring_scatter(backward[1], first[1]).astype(BF16), "xl", 1)
    grad_projected = ring_scatter(backward[0], first[0]) + away.astype(F32)
    grad_lin = col_coef[:, None] * grad_projected
    grad_var = dot(grad_lin, msg_weight.T)
    return (con_update, grad_con, grad_var, weights[1], weights[0])


def solution(mesh):
    fine = Mesh(np.asarray(mesh.devices).reshape(tuple(AXES.values())), tuple(AXES))
    cg, vg = ("z", "xl"), ("xh", "y", "c")
    in_specs = (
        P(cg + vg, None),
        P(vg + cg, None),
        P(cg + vg),
        P(vg + cg),
        P(),
        P(),
        P(),
        P(cg, vg, None),
        P(cg, vg, None),
        P(cg, vg, None, None, None),
        P(cg + vg, None),
    )
    out_specs = (P(cg + vg, None), P(cg + vg, None), P(vg + cg, None), P(), P())
    return jax.shard_map(body, mesh=fine, in_specs=in_specs, out_specs=out_specs, check_vma=False)
```

```python
import functools
import math

import jax
import jax.numpy as jnp
import numpy as np
from jax import lax
from jax.experimental import pallas as pl
from jax.experimental.pallas import tpu as pltpu
from jax.sharding import Mesh
from jax.sharding import PartitionSpec as P

H = 128
TB = 512
AXES = {"z": 8, "xl": 2, "xh": 2, "y": 4, "c": 2}
BF16 = jnp.bfloat16
F32 = jnp.float32


def shift(x, axis, by):
    n = AXES[axis]
    return lax.ppermute(x, axis, [(i, (i + by) % n) for i in range(n)])


def swap(x, axis, mask):
    return lax.ppermute(x, axis, [(i, i ^ mask) for i in range(AXES[axis])])


def ring_gather(x):
    half = x.shape[0] // 2
    parts = [(0, x)]
    up = down = x
    for step in (1, 2, 3):
        up, down = shift(up, "z", 1), shift(down, "z", -1)
        parts += [(2 * (8 - step), up), (2 * step, down)]
    parts += [(8, shift(up[:half], "z", 1)), (9, shift(down[half:], "z", -1))]
    return parts


def pair_start(x):
    up, down = shift(x, "z", 1), shift(x, "z", -1)
    more = shift(up, "z", 1), shift(down, "z", -1)
    return [(0, 0, x), (7, 0, up), (1, 0, down)], more


def pair_end(parts, up, down):
    parts = parts + [(6, 0, up), (2, 0, down)]
    up, down = shift(up, "z", 1), shift(down, "z", -1)
    parts += [(5, 0, up), (3, 0, down)]
    return parts + [(4, 0, shift(up[:1], "z", 1)), (4, 1, shift(down[1:], "z", -1))]


TREE = (("c", 1), ("xl", 1), ("xh", 1), ("y", 1), ("y", 2), ("z", 1), ("z", 2), ("z", 4))


def slot_kernel(side, step, sums, up, down, mine, theirs, *refs):
    outs, (block, sems) = refs[:-2], refs[-2:]
    steps = (step, 8 - step) if step else (0,)
    copies = [
        pltpu.make_async_copy(sums.at[side, p], block.at[i], sems.at[i])
        for i, p in enumerate(steps)
    ]
    for copy in copies:
        copy.start()
    outs[-1][...] = mine[...] + theirs[...]
    for copy in copies:
        copy.wait()
    rows = block.shape[1]
    if step == 0:
        total = block[0] + up[...].astype(F32) + down[...].astype(F32)
        outs[0][...] = total.astype(outs[0].dtype)
    elif step == 3:
        half = rows // 2
        low, high = pl.ds(0, half), pl.ds(half, half)
        outs[0][low] = (block[0, low] + up[...].astype(F32)).astype(BF16)
        outs[0][high] = block[0, high].astype(BF16)
        outs[1][low] = block[1, low].astype(BF16)
        outs[1][high] = (block[1, high] + down[...].astype(F32)).astype(BF16)
    else:
        outs[0][...] = (block[0] + up[...].astype(F32)).astype(BF16)
        outs[1][...] = (block[1] + down[...].astype(F32)).astype(BF16)


def slot(sums, side, step, up, down, mine, theirs):
    rows = sums.shape[2]
    if step:
        out = [jax.ShapeDtypeStruct((rows, H), BF16)] * 2
    else:
        out = [jax.ShapeDtypeStruct((rows, H), BF16 if side else F32)]
    out.append(jax.ShapeDtypeStruct(mine.shape, F32))
    return pl.pallas_call(
        functools.partial(slot_kernel, side, step),
        out_shape=tuple(out),
        in_specs=[ANY_SPEC] + [VMEM_SPEC] * 4,
        out_specs=tuple([VMEM_SPEC] * len(out)),
        scratch_shapes=[pltpu.VMEM((2, rows, H), F32), pltpu.SemaphoreType.DMA((2,))],
        compiler_params=pltpu.CompilerParams(vmem_limit_bytes=8 << 20),
        cost_estimate=pl.CostEstimate(
            flops=2 * rows * H, bytes_accessed=8 * rows * H, transcendentals=0
        ),
        name="slot",
    )(sums, up, down, mine, theirs)


def scatter_and_sum(sums, first, weights):
    half = sums.shape[2] // 2
    links = {}
    for side in (1, 0):
        links[side] = shift(first[side, :half], "z", 1), shift(first[side, half:], "z", -1)
    last = {}
    tree = iter(TREE)
    theirs = swap(weights, *next(tree))
    for step in (3, 2, 1, 0):
        for side in (1, 0):
            *ends, weights = slot(sums, side, step, *links[side], weights, theirs)
            if step:
                links[side] = shift(ends[0], "z", 1), shift(ends[1], "z", -1)
            else:
                last[side] = ends[0]
            if side or step:
                theirs = swap(weights, *next(tree))
        if step == 0:
            break
    return last[0] + swap(last[1], "xl", 1).astype(F32), weights


GRANT = 57 << 20
ANY_SPEC = pl.BlockSpec(memory_space=pl.ANY)
VMEM_SPEC = pl.BlockSpec(memory_space=pltpu.VMEM)


def each_tile(put, base, blocks, action):
    def step(k, carry):
        place = put[k] - base

        @pl.when((place >= 0) & (place < blocks))
        def _():
            action(k, place)

        return carry

    lax.fori_loop(0, put.shape[0], step, 0)


def add_products(take, put, copies, source, tiles, held, tile_sem, total, base, transpose):
    blocks = total.shape[0] // TB

    def fetch(k):
        return pltpu.make_async_copy(tiles.at[k], held.at[k], tile_sem.at[k])

    for copy in copies:
        copy.start()
    each_tile(put, base, blocks, lambda k, place: fetch(k).start())

    def clear(k, carry):
        total[pl.ds(pl.multiple_of(k * TB, TB), TB), :] = jnp.zeros((TB, H), F32)
        return carry

    lax.fori_loop(0, blocks, clear, 0)
    for copy in copies:
        copy.wait()

    def multiply(k, place):
        fetch(k).wait()
        rows = source[pl.ds(pl.multiple_of(take[k] * TB, TB), TB), :]
        width = TB // 2
        for part in range(2):
            cut = pl.ds(part * width, width)
            if transpose:
                product = lax.dot_general(
                    held[k, :, cut], rows, (((0,), (0,)), ((), ())), preferred_element_type=F32
                )
            else:
                product = jnp.dot(held[k, cut, :], rows, preferred_element_type=F32)
            at = pl.ds(pl.multiple_of(place * TB + part * width, width), width)
            total[at, :] += product

    each_tile(put, base, blocks, multiply)


def forward_kernel(places, take, put, *refs):
    n = len(places)
    sources, (tiles, near, far, source, held, total, source_sem, tile_sem, out_sem) = refs[:n], refs[n:]
    copies = [
        pltpu.make_async_copy(
            ref, source.at[pl.ds(place * TB, ref.shape[0])], source_sem.at[i]
        )
        for i, (place, ref) in enumerate(zip(places, sources, strict=True))
    ]
    add_products(take, put, copies, source, tiles, held, tile_sem, total, 0, False)
    half = near.shape[0]
    out = pltpu.make_async_copy(total.at[pl.ds(0, half)], near, out_sem)
    out.start()

    def store(k, carry):
        at = pl.multiple_of(k * TB, TB)
        far[pl.ds(at, TB), :] = total[pl.ds(half + at, TB), :].astype(BF16)
        return carry

    lax.fori_loop(0, half // TB, store, 0)
    out.wait()


def tiles_forward(parts, take, put, tiles):
    arrays = [array for _, array in parts]
    count = tiles.shape[0]
    return pl.pallas_call(
        functools.partial(forward_kernel, tuple(place for place, _ in parts)),
        out_shape=(
            jax.ShapeDtypeStruct((16 * TB, H), F32),
            jax.ShapeDtypeStruct((16 * TB, H), BF16),
        ),
        grid_spec=pltpu.PrefetchScalarGridSpec(
            num_scalar_prefetch=2,
            grid=(),
            in_specs=[ANY_SPEC] * (len(arrays) + 1),
            out_specs=(ANY_SPEC, VMEM_SPEC),
            scratch_shapes=[
                pltpu.VMEM((32 * TB, H), BF16),
                pltpu.VMEM((count, TB, TB), BF16),
                pltpu.VMEM((32 * TB, H), F32),
                pltpu.SemaphoreType.DMA((len(arrays),)),
                pltpu.SemaphoreType.DMA((count,)),
                pltpu.SemaphoreType.DMA,
            ],
        ),
        compiler_params=pltpu.CompilerParams(vmem_limit_bytes=GRANT),
        cost_estimate=pl.CostEstimate(
            flops=2 * tiles.size * H, bytes_accessed=2 * tiles.size + 32 * TB * H * 5, transcendentals=0
        ),
        name="tiles_forward",
    )(take, put, *arrays, tiles)


def back_kernel(places, take, put, own, other, tiles, *refs):
    n = len(places)
    scaled, (sums, first, weight, source, held, total, right, sems, tile_sem, load_sem) = refs[:n], refs[n:]
    half = own.shape[0]
    ins = [
        pltpu.make_async_copy(own, source.at[pl.ds(0, half)], sems.at[0]),
        pltpu.make_async_copy(other, source.at[pl.ds(half, half)], sems.at[1]),
    ]
    loads = [
        pltpu.make_async_copy(ref, right.at[pl.ds(side, ref.shape[0]), place], load_sem.at[i])
        for i, ((place, side), ref) in enumerate(zip(places, scaled, strict=True))
    ]
    add_products(take, put, ins, source, tiles, held, tile_sem, total, 0, True)
    out = pltpu.make_async_copy(total, sums, sems.at[2])
    out.start()
    for load in loads:
        load.start()
    rows = first.shape[1]
    for side in range(2):
        first[side] = total[pl.ds((side * 8 + 4) * rows, rows), :].astype(BF16)
    for load in loads:
        load.wait()

    def contract(k, carry):
        block = total[pl.ds(pl.multiple_of(k * rows, rows), rows), :]
        high = block.astype(BF16)
        low = (block - high.astype(F32)).astype(BF16)
        both = lax.dot_general(
            right[k // 8, k % 8],
            jnp.concatenate([high, low], axis=1),
            (((0,), (0,)), ((), ())),
            preferred_element_type=F32,
        )
        return carry + both[:, :H] + both[:, H:]

    weight[...] = lax.fori_loop(0, 16, contract, jnp.zeros(weight.shape, F32))
    out.wait()


def tiles_back(own, other, take, put, tiles, scaled):
    arrays = [array for _, _, array in scaled]
    rows, count = arrays[0].shape[1], tiles.shape[0]
    return pl.pallas_call(
        functools.partial(back_kernel, tuple((place, side) for place, side, _ in scaled)),
        out_shape=(
            jax.ShapeDtypeStruct((16 * rows, H), F32),
            jax.ShapeDtypeStruct((2, rows, H), BF16),
            jax.ShapeDtypeStruct((H, H), F32),
        ),
        grid_spec=pltpu.PrefetchScalarGridSpec(
            num_scalar_prefetch=2,
            grid=(),
            in_specs=[ANY_SPEC] * (3 + len(arrays)),
            out_specs=(ANY_SPEC, VMEM_SPEC, VMEM_SPEC),
            scratch_shapes=[
                pltpu.VMEM((16 * rows, H), BF16),
                pltpu.VMEM((count, TB, TB), BF16),
                pltpu.VMEM((16 * rows, H), F32),
                pltpu.VMEM((2, 8, rows, H), BF16),
                pltpu.SemaphoreType.DMA((3,)),
                pltpu.SemaphoreType.DMA((count,)),
                pltpu.SemaphoreType.DMA((len(arrays),)),
            ],
        ),
        compiler_params=pltpu.CompilerParams(vmem_limit_bytes=GRANT),
        cost_estimate=pl.CostEstimate(
            flops=2 * tiles.size * H, bytes_accessed=2 * tiles.size + 32 * TB * H * 8, transcendentals=0
        ),
        name="tiles_back",
    )(take, put, own, other, tiles, *arrays)


def body(
    con_embed,
    var_embed,
    row_coef,
    col_coef,
    self_weight,
    msg_weight,
    timestep,
    tile_rows,
    tile_cols,
    pattern,
    cotangent,
):
    dot = functools.partial(
        jnp.dot, precision=lax.Precision.HIGHEST, preferred_element_type=F32
    )
    rows_here = con_embed.shape[0]
    z, xl, core = lax.axis_index("z"), lax.axis_index("xl"), lax.axis_index("c")
    tiles = pattern.reshape(-1, TB, TB)
    row, col = tile_rows.reshape(-1), tile_cols.reshape(-1)
    row_owner, col_owner = row // 2, col // 2
    row_at = (((row_owner % 2) ^ core) * 8 + row_owner // 2) * 2 + row % 2
    col_at = (((col_owner % 2) ^ xl) * 8 + (col_owner // 2 - z) % 8) * 2 + col % 2

    projected = (dot(var_embed, msg_weight) * col_coef[:, None]).astype(BF16)
    near = ring_gather(projected)
    far = ring_gather(swap(projected, "xl", 1))
    parts = near + [(16 + place, array) for place, array in far]
    partial, sibling = tiles_forward(parts, col_at, row_at, tiles)
    scaled = (var_embed * col_coef[:, None]).astype(BF16)
    scaled = jnp.stack([scaled, swap(scaled, "xl", 1)])
    sibling, scaled = lax.optimization_barrier((sibling, scaled))
    sibling = swap(sibling, "c", 1)
    scaled, more = pair_start(scaled)
    partial = (partial + sibling.astype(F32)).astype(BF16)
    partial = partial.reshape(8, rows_here, H)
    partial = lax.all_to_all(partial, ("xh", "y"), split_axis=0, concat_axis=0, tiled=True)
    partial, more = lax.optimization_barrier((partial, more))
    scaled = pair_end(scaled, *more)
    messages = jnp.sum(partial.astype(F32), axis=0)

    frequency = jnp.exp(-math.log(10000.0) * jnp.arange(H // 2, dtype=F32) / (H // 2))
    phases = timestep[0].astype(F32) * frequency
    time_embed = jnp.concatenate([jnp.sin(phases), jnp.cos(phases)])
    preact = dot(con_embed, self_weight) + row_coef[:, None] * messages + time_embed[None, :]
    sigmoid_z = jax.nn.sigmoid(preact)
    con_update = con_embed + preact * sigmoid_z
    grad_pre = cotangent * sigmoid_z * (1.0 + preact * (1.0 - sigmoid_z))
    grad_messages = (row_coef[:, None] * grad_pre).astype(BF16)

    copies = jnp.broadcast_to(grad_messages[None], (8, rows_here, H))
    own = lax.all_to_all(copies, ("xh", "y"), split_axis=0, concat_axis=0, tiled=True)
    own, blocks = lax.optimization_barrier((own, [block for _, _, block in scaled]))
    scaled = [(place, side, block) for (place, side, _), block in zip(scaled, blocks, strict=True)]
    own = own.reshape(8 * rows_here, H)
    other = swap(own, "c", 1)
    grad_con = cotangent + dot(grad_pre, self_weight.T)
    local_self = dot(con_embed.T, grad_pre)
    backward, first, local_msg = tiles_back(own, other, row_at, col_at, tiles, scaled)
    backward = backward.reshape(2, 8, rows_here, H)
    grad_projected, weights = scatter_and_sum(backward, first, jnp.stack([local_self, local_msg]))
    grad_lin = col_coef[:, None] * grad_projected
    grad_var = dot(grad_lin, msg_weight.T)
    return (con_update, grad_con, grad_var, weights[1], weights[0])


def solution(mesh):
    fine = Mesh(np.asarray(mesh.devices).reshape(tuple(AXES.values())), tuple(AXES))
    cg, vg = ("z", "xl"), ("xh", "y", "c")
    in_specs = (
        P(cg + vg, None),
        P(vg + cg, None),
        P(cg + vg),
        P(vg + cg),
        P(),
        P(),
        P(),
        P(cg, vg, None),
        P(cg, vg, None),
        P(cg, vg, None, None, None),
        P(cg + vg, None),
    )
    out_specs = (P(cg + vg, None), P(cg + vg, None), P(vg + cg, None), P(), P())
    return jax.shard_map(body, mesh=fine, in_specs=in_specs, out_specs=out_specs, check_vma=False)
```

```python
import functools
import math

import jax
import jax.numpy as jnp
import numpy as np
from jax import lax
from jax.experimental import pallas as pl
from jax.experimental.pallas import tpu as pltpu
from jax.sharding import Mesh
from jax.sharding import PartitionSpec as P

H = 128
TB = 512
AXES = {"z": 8, "xl": 2, "xh": 2, "y": 4, "c": 2}
BF16 = jnp.bfloat16
F32 = jnp.float32


def shift(x, axis, by):
    n = AXES[axis]
    return lax.ppermute(x, axis, [(i, (i + by) % n) for i in range(n)])


def swap(x, axis, mask):
    return lax.ppermute(x, axis, [(i, i ^ mask) for i in range(AXES[axis])])


def ring_gather(x):
    half = x.shape[0] // 2
    parts = [(0, x)]
    up = down = x
    for step in (1, 2, 3):
        up, down = shift(up, "z", 1), shift(down, "z", -1)
        parts += [(2 * (8 - step), up), (2 * step, down)]
    parts += [(8, shift(up[:half], "z", 1)), (9, shift(down[half:], "z", -1))]
    return parts


def pair_start(x):
    up, down = shift(x, "z", 1), shift(x, "z", -1)
    more = shift(up, "z", 1), shift(down, "z", -1)
    return [(0, 0, x), (7, 0, up), (1, 0, down)], more


def pair_end(parts, up, down):
    parts = parts + [(6, 0, up), (2, 0, down)]
    up, down = shift(up, "z", 1), shift(down, "z", -1)
    parts += [(5, 0, up), (3, 0, down)]
    return parts + [(4, 0, shift(up[:1], "z", 1)), (4, 1, shift(down[1:], "z", -1))]


TREE = (("c", 1), ("xl", 1), ("xh", 1), ("y", 1), ("y", 2), ("z", 1), ("z", 2), ("z", 4))


def slot_kernel(side, step, sums, up, down, *refs):
    outs, (block, sems) = refs[:-2], refs[-2:]
    if (side, step) != (1, 3):
        (mine, theirs), outs = outs[:2], outs[2:]
    steps = (step, 8 - step) if step else (0,)
    copies = [
        pltpu.make_async_copy(sums.at[side, p], block.at[i], sems.at[i])
        for i, p in enumerate(steps)
    ]
    for copy in copies:
        copy.start()
    if (side, step) != (1, 3):
        outs[-1][...] = mine[...] + theirs[...]
    for copy in copies:
        copy.wait()
    rows = block.shape[1]
    if step == 0:
        total = block[0] + up[...].astype(F32) + down[...].astype(F32)
        outs[0][...] = total.astype(outs[0].dtype)
    elif step == 3:
        half = rows // 2
        low, high = pl.ds(0, half), pl.ds(half, half)
        outs[0][low] = (block[0, low] + up[...].astype(F32)).astype(BF16)
        outs[0][high] = block[0, high].astype(BF16)
        outs[1][low] = block[1, low].astype(BF16)
        outs[1][high] = (block[1, high] + down[...].astype(F32)).astype(BF16)
    else:
        outs[0][...] = (block[0] + up[...].astype(F32)).astype(BF16)
        outs[1][...] = (block[1] + down[...].astype(F32)).astype(BF16)


def slot(sums, side, step, up, down, *tree):
    rows = sums.shape[2]
    if step:
        out = [jax.ShapeDtypeStruct((rows, H), BF16)] * 2
    else:
        out = [jax.ShapeDtypeStruct((rows, H), BF16 if side else F32)]
    out += [jax.ShapeDtypeStruct(x.shape, F32) for x in tree[:1]]
    return pl.pallas_call(
        functools.partial(slot_kernel, side, step),
        out_shape=tuple(out),
        in_specs=[ANY_SPEC] + [VMEM_SPEC] * (2 + len(tree)),
        out_specs=tuple([VMEM_SPEC] * len(out)),
        scratch_shapes=[pltpu.VMEM((2, rows, H), F32), pltpu.SemaphoreType.DMA((2,))],
        compiler_params=pltpu.CompilerParams(vmem_limit_bytes=8 << 20),
        cost_estimate=pl.CostEstimate(
            flops=2 * rows * H, bytes_accessed=8 * rows * H, transcendentals=0
        ),
        name="slot",
    )(sums, up, down, *tree)


def scatter_and_sum(sums, first, weights):
    half = sums.shape[2] // 2
    links, last = {}, {}
    for side in (1, 0):
        links[side] = (
            shift(first[side, :half], "z", 1),
            shift(first[side, half:], "z", -1),
        )
    tree = iter(TREE)
    theirs = None
    for step in (3, 2, 1, 0):
        for side in (1, 0):
            if theirs is None:
                ends = slot(sums, side, step, *links[side])
            else:
                *ends, weights = slot(sums, side, step, *links[side], weights, theirs)
            if step:
                links[side] = shift(ends[0], "z", 1), shift(ends[1], "z", -1)
            else:
                last[side] = ends[0]
            theirs = swap(weights, *next(tree))
    return last[0] + swap(last[1], "xl", 1).astype(F32), weights + theirs


GRANT = 24 << 20
HOLD_GRANT = 44 << 20
ANY_SPEC = pl.BlockSpec(memory_space=pl.ANY)
VMEM_SPEC = pl.BlockSpec(memory_space=pltpu.VMEM)


def hold_kernel(tiles, token, held, sem):
    copy = pltpu.make_async_copy(tiles, held, sem)
    copy.start()
    copy.wait()


def hold(tiles, token):
    return pl.pallas_call(
        hold_kernel,
        out_shape=jax.ShapeDtypeStruct(tiles.shape, tiles.dtype),
        in_specs=[ANY_SPEC, ANY_SPEC],
        out_specs=VMEM_SPEC,
        scratch_shapes=[pltpu.SemaphoreType.DMA],
        compiler_params=pltpu.CompilerParams(vmem_limit_bytes=HOLD_GRANT),
        cost_estimate=pl.CostEstimate(
            flops=0, bytes_accessed=4 * tiles.size, transcendentals=0
        ),
        name="hold_tiles",
    )(tiles, token)


def add_products(take, put, copies, source, held, total, transpose):
    for copy in copies:
        copy.start()

    def clear(k, carry):
        total[pl.ds(pl.multiple_of(k * TB, TB), TB), :] = jnp.zeros((TB, H), F32)
        return carry

    lax.fori_loop(0, total.shape[0] // TB, clear, 0)
    for copy in copies:
        copy.wait()

    def multiply(k, carry):
        rows = source[pl.ds(pl.multiple_of(take[k] * TB, TB), TB), :]
        target = pl.multiple_of(put[k] * TB, TB)
        width = TB // 2
        for part in range(2):
            cut = pl.ds(part * width, width)
            if transpose:
                product = lax.dot_general(
                    held[k, :, cut], rows, (((0,), (0,)), ((), ())), preferred_element_type=F32
                )
            else:
                product = jnp.dot(held[k, cut, :], rows, preferred_element_type=F32)
            at = pl.ds(pl.multiple_of(target + part * width, width), width)
            total[at, :] += product
        return carry

    lax.fori_loop(0, held.shape[0], multiply, 0)


def tile_kernel(places, transpose, take, put, *refs):
    n = len(places)
    sources, held, outs, (source, sems) = refs[:n], refs[n], refs[n + 1 : -2], refs[-2:]
    total = outs[0]
    copies = [
        pltpu.make_async_copy(ref, source.at[pl.ds(place * TB, ref.shape[0])], sems.at[i])
        for i, (place, ref) in enumerate(zip(places, sources, strict=True))
    ]
    add_products(take, put, copies, source, held, total, transpose)
    for first in outs[1:]:
        rows = first.shape[1]
        for side in range(2):
            first[side] = total[pl.ds((side * 8 + 4) * rows, rows), :].astype(BF16)


def tile_products(parts, take, put, held, blocks, transpose):
    arrays = [array for _, array in parts]
    out = [jax.ShapeDtypeStruct((blocks * TB, H), F32)]
    if transpose:
        out.append(jax.ShapeDtypeStruct((2, blocks * TB // 16, H), BF16))
    return pl.pallas_call(
        functools.partial(tile_kernel, tuple(place for place, _ in parts), transpose),
        out_shape=tuple(out),
        grid_spec=pltpu.PrefetchScalarGridSpec(
            num_scalar_prefetch=2,
            grid=(),
            in_specs=[ANY_SPEC] * len(arrays) + [VMEM_SPEC],
            out_specs=tuple([VMEM_SPEC] * len(out)),
            scratch_shapes=[
                pltpu.VMEM((blocks * TB, H), BF16),
                pltpu.SemaphoreType.DMA((len(arrays),)),
            ],
        ),
        compiler_params=pltpu.CompilerParams(vmem_limit_bytes=GRANT),
        cost_estimate=pl.CostEstimate(
            flops=2 * held.size * H, bytes_accessed=2 * held.size + blocks * TB * H * 6, transcendentals=0
        ),
        name="tiles_back" if transpose else "tiles_forward",
    )(take, put, *arrays, held)


def weight_kernel(places, sums, *refs):
    n = len(places)
    scaled, (out,) = refs[:n], refs[n:]
    out[...] = jnp.zeros_like(out)
    for (place, side), ref in zip(places, scaled, strict=True):
        for i in range(ref.shape[0]):
            block = sums[side + i, place]
            high = block.astype(BF16)
            low = (block - high.astype(F32)).astype(BF16)
            both = lax.dot_general(
                ref[i],
                jnp.concatenate([high, low], axis=1),
                (((0,), (0,)), ((), ())),
                preferred_element_type=F32,
            )
            out[...] += both[:, :H] + both[:, H:]


def weight_partial(sums, scaled):
    arrays = [array for _, _, array in scaled]
    return pl.pallas_call(
        functools.partial(weight_kernel, tuple((place, side) for place, side, _ in scaled)),
        out_shape=jax.ShapeDtypeStruct((H, H), F32),
        in_specs=[VMEM_SPEC] * (1 + len(arrays)),
        out_specs=VMEM_SPEC,
        compiler_params=pltpu.CompilerParams(vmem_limit_bytes=GRANT),
        cost_estimate=pl.CostEstimate(
            flops=4 * sums.size * H, bytes_accessed=6 * sums.size, transcendentals=0
        ),
        name="weight_partial",
    )(sums, *arrays)


def body(
    con_embed,
    var_embed,
    row_coef,
    col_coef,
    self_weight,
    msg_weight,
    timestep,
    tile_rows,
    tile_cols,
    pattern,
    cotangent,
):
    dot = functools.partial(
        jnp.dot, precision=lax.Precision.HIGHEST, preferred_element_type=F32
    )
    rows_here = con_embed.shape[0]
    z, xl, core = lax.axis_index("z"), lax.axis_index("xl"), lax.axis_index("c")
    tiles = pattern.reshape(-1, TB, TB)
    row, col = tile_rows.reshape(-1), tile_cols.reshape(-1)
    row_owner, col_owner = row // 2, col // 2
    row_at = (((row_owner % 2) ^ core) * 8 + row_owner // 2) * 2 + row % 2
    col_at = (((col_owner % 2) ^ xl) * 8 + (col_owner // 2 - z) % 8) * 2 + col % 2

    projected = (dot(var_embed, msg_weight) * col_coef[:, None]).astype(BF16)
    near = ring_gather(projected)
    far = ring_gather(swap(projected, "xl", 1))
    parts = near + [(16 + place, array) for place, array in far]
    (forward,) = tile_products(parts, col_at, row_at, hold(tiles, near[5][1]), 32, False)
    forward = forward.reshape(2, 8 * rows_here, H)
    scaled = (var_embed * col_coef[:, None]).astype(BF16)
    scaled = jnp.stack([scaled, swap(scaled, "xl", 1)])
    forward, scaled = lax.optimization_barrier((forward, scaled))
    sibling = swap(forward[1].astype(BF16), "c", 1)
    scaled, more = pair_start(scaled)
    partial = (forward[0] + sibling.astype(F32)).astype(BF16)
    partial = partial.reshape(8, rows_here, H)
    partial = lax.all_to_all(partial, ("xh", "y"), split_axis=0, concat_axis=0, tiled=True)
    partial, more = lax.optimization_barrier((partial, more))
    scaled = pair_end(scaled, *more)
    messages = jnp.sum(partial.astype(F32), axis=0)

    frequency = jnp.exp(-math.log(10000.0) * jnp.arange(H // 2, dtype=F32) / (H // 2))
    phases = timestep[0].astype(F32) * frequency
    time_embed = jnp.concatenate([jnp.sin(phases), jnp.cos(phases)])
    preact = dot(con_embed, self_weight) + row_coef[:, None] * messages + time_embed[None, :]
    sigmoid_z = jax.nn.sigmoid(preact)
    con_update = con_embed + preact * sigmoid_z
    grad_pre = cotangent * sigmoid_z * (1.0 + preact * (1.0 - sigmoid_z))
    grad_messages = (row_coef[:, None] * grad_pre).astype(BF16)

    copies = jnp.broadcast_to(grad_messages[None], (8, rows_here, H))
    own = lax.all_to_all(copies, ("xh", "y"), split_axis=0, concat_axis=0, tiled=True)
    own, blocks = lax.optimization_barrier((own, [block for _, _, block in scaled]))
    scaled = [(place, side, block) for (place, side, _), block in zip(scaled, blocks, strict=True)]
    own = own.reshape(8 * rows_here, H)
    other = swap(own, "c", 1)
    grad_con = cotangent + dot(grad_pre, self_weight.T)
    local_self = dot(con_embed.T, grad_pre)
    held = hold(tiles, grad_messages)
    backward, first = tile_products([(0, own), (16, other)], row_at, col_at, held, 32, True)
    backward = backward.reshape(2, 8, rows_here, H)
    local_msg = weight_partial(backward, scaled)
    grad_projected, weights = scatter_and_sum(backward, first, jnp.stack([local_self, local_msg]))
    grad_lin = col_coef[:, None] * grad_projected
    grad_var = dot(grad_lin, msg_weight.T)
    return (con_update, grad_con, grad_var, weights[1], weights[0])


def solution(mesh):
    fine = Mesh(np.asarray(mesh.devices).reshape(tuple(AXES.values())), tuple(AXES))
    cg, vg = ("z", "xl"), ("xh", "y", "c")
    in_specs = (
        P(cg + vg, None),
        P(vg + cg, None),
        P(cg + vg),
        P(vg + cg),
        P(),
        P(),
        P(),
        P(cg, vg, None),
        P(cg, vg, None),
        P(cg, vg, None, None, None),
        P(cg + vg, None),
    )
    out_specs = (P(cg + vg, None), P(cg + vg, None), P(vg + cg, None), P(), P())
    return jax.shard_map(body, mesh=fine, in_specs=in_specs, out_specs=out_specs, check_vma=False)
```

```python
import functools
import math

import jax
import jax.numpy as jnp
import numpy as np
from jax import lax
from jax.experimental import pallas as pl
from jax.experimental.pallas import tpu as pltpu
from jax.sharding import Mesh
from jax.sharding import PartitionSpec as P

H = 128
TB = 512
AXES = {"z": 8, "xl": 2, "xh": 2, "y": 4, "c": 2}
BF16 = jnp.bfloat16
F32 = jnp.float32


def shift(x, axis, by):
    n = AXES[axis]
    return lax.ppermute(x, axis, [(i, (i + by) % n) for i in range(n)])


def swap(x, axis, mask):
    return lax.ppermute(x, axis, [(i, i ^ mask) for i in range(AXES[axis])])


def ring_gather(x):
    half = x.shape[0] // 2
    parts = [(0, x)]
    up = down = x
    for step in (1, 2, 3):
        up, down = shift(up, "z", 1), shift(down, "z", -1)
        parts += [(2 * (8 - step), up), (2 * step, down)]
    parts += [(8, shift(up[:half], "z", 1)), (9, shift(down[half:], "z", -1))]
    return parts


def pair_start(x):
    up, down = shift(x, "z", 1), shift(x, "z", -1)
    more = shift(up, "z", 1), shift(down, "z", -1)
    return [(0, 0, x), (7, 0, up), (1, 0, down)], more


def pair_end(parts, up, down):
    parts = parts + [(6, 0, up), (2, 0, down)]
    up, down = shift(up, "z", 1), shift(down, "z", -1)
    parts += [(5, 0, up), (3, 0, down)]
    return parts + [(4, 0, shift(up[:1], "z", 1)), (4, 1, shift(down[1:], "z", -1))]


TREE = (("z", 4), ("z", 2), ("z", 1), ("xh", 1), ("y", 2), ("y", 1), ("xl", 1))


def slot_kernel(side, step, sums, up, down, *refs):
    outs, (block, sems) = refs[:-2], refs[-2:]
    if (side, step) != (1, 3):
        (mine, theirs), outs = outs[:2], outs[2:]
    steps = (step, 8 - step) if step else (0,)
    copies = [
        pltpu.make_async_copy(sums.at[side, p], block.at[i], sems.at[i])
        for i, p in enumerate(steps)
    ]
    for copy in copies:
        copy.start()
    if (side, step) != (1, 3):
        outs[-1][...] = mine[...] + theirs[...]
    for copy in copies:
        copy.wait()
    rows = block.shape[1]
    if step == 0:
        total = block[0] + up[...].astype(F32) + down[...].astype(F32)
        outs[0][...] = total.astype(outs[0].dtype)
    elif step == 3:
        half = rows // 2
        low, high = pl.ds(0, half), pl.ds(half, half)
        outs[0][low] = (block[0, low] + up[...].astype(F32)).astype(BF16)
        outs[0][high] = block[0, high].astype(BF16)
        outs[1][low] = block[1, low].astype(BF16)
        outs[1][high] = (block[1, high] + down[...].astype(F32)).astype(BF16)
    else:
        outs[0][...] = (block[0] + up[...].astype(F32)).astype(BF16)
        outs[1][...] = (block[1] + down[...].astype(F32)).astype(BF16)


def slot(sums, side, step, up, down, *tree):
    rows = sums.shape[2]
    if step:
        out = [jax.ShapeDtypeStruct((rows, H), BF16)] * 2
    else:
        out = [jax.ShapeDtypeStruct((rows, H), BF16 if side else F32)]
    out += [jax.ShapeDtypeStruct(x.shape, F32) for x in tree[:1]]
    return pl.pallas_call(
        functools.partial(slot_kernel, side, step),
        out_shape=tuple(out),
        in_specs=[ANY_SPEC] + [VMEM_SPEC] * (2 + len(tree)),
        out_specs=tuple([VMEM_SPEC] * len(out)),
        scratch_shapes=[pltpu.VMEM((2, rows, H), F32), pltpu.SemaphoreType.DMA((2,))],
        compiler_params=pltpu.CompilerParams(vmem_limit_bytes=8 << 20),
        cost_estimate=pl.CostEstimate(
            flops=2 * rows * H, bytes_accessed=8 * rows * H, transcendentals=0
        ),
        name="slot",
    )(sums, up, down, *tree)


def scatter_and_sum(sums, first, weights):
    half = sums.shape[2] // 2
    links, last = {}, {}
    for side in (1, 0):
        links[side] = shift(first[side, :half], "z", 1), shift(first[side, half:], "z", -1)
    lead = lax.axis_index("c") == 0
    mine = jnp.where(lead, weights[0], weights[1])
    mine = mine + swap(jnp.where(lead, weights[1], weights[0]), "c", 1)
    tree = iter(TREE)
    theirs = None
    for step in (3, 2, 1, 0):
        for side in (1, 0):
            if theirs is None:
                ends = slot(sums, side, step, *links[side])
            else:
                *ends, mine = slot(sums, side, step, *links[side], mine, theirs)
            if step:
                links[side] = shift(ends[0], "z", 1), shift(ends[1], "z", -1)
            else:
                last[side] = ends[0]
            if side or step:
                theirs = swap(mine, *next(tree))
    theirs = swap(mine, "c", 1)
    total = last[0] + swap(last[1], "xl", 1).astype(F32)
    return total, jnp.where(lead, mine, theirs), jnp.where(lead, theirs, mine)


GRANT = 24 << 20
HOLD_GRANT = 40 << 20
ANY_SPEC = pl.BlockSpec(memory_space=pl.ANY)
VMEM_SPEC = pl.BlockSpec(memory_space=pltpu.VMEM)


def hold_kernel(tiles, token, held, sem):
    copy = pltpu.make_async_copy(tiles, held, sem)
    copy.start()
    copy.wait()


def hold(tiles, token):
    return pl.pallas_call(
        hold_kernel,
        out_shape=jax.ShapeDtypeStruct(tiles.shape, tiles.dtype),
        in_specs=[ANY_SPEC, ANY_SPEC],
        out_specs=VMEM_SPEC,
        scratch_shapes=[pltpu.SemaphoreType.DMA],
        compiler_params=pltpu.CompilerParams(vmem_limit_bytes=HOLD_GRANT),
        cost_estimate=pl.CostEstimate(
            flops=0, bytes_accessed=4 * tiles.size, transcendentals=0
        ),
        name="hold_tiles",
    )(tiles, token)


def add_products(take, put, copies, source, held, total, transpose):
    for copy in copies:
        copy.start()

    def clear(k, carry):
        total[pl.ds(pl.multiple_of(k * TB, TB), TB), :] = jnp.zeros((TB, H), F32)
        return carry

    lax.fori_loop(0, total.shape[0] // TB, clear, 0)
    for copy in copies:
        copy.wait()

    def multiply(k, carry):
        rows = source[pl.ds(pl.multiple_of(take[k] * TB, TB), TB), :]
        target = pl.multiple_of(put[k] * TB, TB)
        width = TB // 2
        for part in range(2):
            cut = pl.ds(part * width, width)
            if transpose:
                product = lax.dot_general(
                    held[k, :, cut], rows, (((0,), (0,)), ((), ())), preferred_element_type=F32
                )
            else:
                product = jnp.dot(held[k, cut, :], rows, preferred_element_type=F32)
            at = pl.ds(pl.multiple_of(target + part * width, width), width)
            total[at, :] += product
        return carry

    lax.fori_loop(0, held.shape[0], multiply, 0)


def tile_kernel(places, transpose, take, put, *refs):
    n = len(places)
    sources, held, outs, (source, sems) = refs[:n], refs[n], refs[n + 1 : -2], refs[-2:]
    total = outs[0]
    copies = [
        pltpu.make_async_copy(ref, source.at[pl.ds(place * TB, ref.shape[0])], sems.at[i])
        for i, (place, ref) in enumerate(zip(places, sources, strict=True))
    ]
    add_products(take, put, copies, source, held, total, transpose)
    for first in outs[1:]:
        rows = first.shape[1]
        for side in range(2):
            first[side] = total[pl.ds((side * 8 + 4) * rows, rows), :].astype(BF16)


def tile_products(parts, take, put, held, blocks, transpose):
    arrays = [array for _, array in parts]
    out = [jax.ShapeDtypeStruct((blocks * TB, H), F32)]
    if transpose:
        out.append(jax.ShapeDtypeStruct((2, blocks * TB // 16, H), BF16))
    return pl.pallas_call(
        functools.partial(tile_kernel, tuple(place for place, _ in parts), transpose),
        out_shape=tuple(out),
        grid_spec=pltpu.PrefetchScalarGridSpec(
            num_scalar_prefetch=2,
            grid=(),
            in_specs=[ANY_SPEC] * len(arrays) + [VMEM_SPEC],
            out_specs=tuple([VMEM_SPEC] * len(out)),
            scratch_shapes=[
                pltpu.VMEM((blocks * TB, H), BF16),
                pltpu.SemaphoreType.DMA((len(arrays),)),
            ],
        ),
        compiler_params=pltpu.CompilerParams(vmem_limit_bytes=GRANT),
        cost_estimate=pl.CostEstimate(
            flops=2 * held.size * H, bytes_accessed=2 * held.size + blocks * TB * H * 6, transcendentals=0
        ),
        name="tiles_back" if transpose else "tiles_forward",
    )(take, put, *arrays, held)


def weight_kernel(places, sums, *refs):
    n = len(places)
    scaled, (out,) = refs[:n], refs[n:]
    out[...] = jnp.zeros_like(out)
    for (place, side), ref in zip(places, scaled, strict=True):
        for i in range(ref.shape[0]):
            block = sums[side + i, place]
            high = block.astype(BF16)
            low = (block - high.astype(F32)).astype(BF16)
            both = lax.dot_general(
                ref[i],
                jnp.concatenate([high, low], axis=1),
                (((0,), (0,)), ((), ())),
                preferred_element_type=F32,
            )
            out[...] += both[:, :H] + both[:, H:]


def weight_partial(sums, scaled):
    arrays = [array for _, _, array in scaled]
    return pl.pallas_call(
        functools.partial(weight_kernel, tuple((place, side) for place, side, _ in scaled)),
        out_shape=jax.ShapeDtypeStruct((H, H), F32),
        in_specs=[VMEM_SPEC] * (1 + len(arrays)),
        out_specs=VMEM_SPEC,
        compiler_params=pltpu.CompilerParams(vmem_limit_bytes=GRANT),
        cost_estimate=pl.CostEstimate(
            flops=4 * sums.size * H, bytes_accessed=6 * sums.size, transcendentals=0
        ),
        name="weight_partial",
    )(sums, *arrays)


def mid_kernel(partial, base, scale, con, cot, update, pre, copies):
    width = 128

    def step(k, carry):
        at = pl.ds(pl.multiple_of(k * width, width), width)
        messages = partial[0, at, :].astype(F32)
        for i in range(1, partial.shape[0]):
            messages += partial[i, at, :].astype(F32)
        preact = base[at, :] + scale[at, :] * messages
        gate = jax.nn.sigmoid(preact)
        update[at, :] = con[at, :] + preact * gate
        grad = cot[at, :] * gate * (1.0 + preact * (1.0 - gate))
        pre[at, :] = grad
        sent = (scale[at, :] * grad).astype(BF16)
        for i in range(copies.shape[0]):
            copies[i, at, :] = sent
        return carry

    lax.fori_loop(0, con.shape[0] // width, step, 0)


def mid(partial, base, scale, con, cot):
    return pl.pallas_call(
        mid_kernel,
        out_shape=(
            jax.ShapeDtypeStruct(con.shape, F32),
            jax.ShapeDtypeStruct(con.shape, F32),
            jax.ShapeDtypeStruct(partial.shape, BF16),
        ),
        in_specs=[VMEM_SPEC] * 5,
        out_specs=(VMEM_SPEC,) * 3,
        compiler_params=pltpu.CompilerParams(vmem_limit_bytes=12 << 20),
        cost_estimate=pl.CostEstimate(
            flops=24 * con.size, bytes_accessed=56 * con.size, transcendentals=con.size
        ),
        name="mid",
    )(partial, base, scale, con, cot)


def body(
    con_embed,
    var_embed,
    row_coef,
    col_coef,
    self_weight,
    msg_weight,
    timestep,
    tile_rows,
    tile_cols,
    pattern,
    cotangent,
):
    dot = functools.partial(
        jnp.dot, precision=lax.Precision.HIGHEST, preferred_element_type=F32
    )
    rows_here = con_embed.shape[0]
    z, xl, core = lax.axis_index("z"), lax.axis_index("xl"), lax.axis_index("c")
    tiles = pattern.reshape(-1, TB, TB)
    row, col = tile_rows.reshape(-1), tile_cols.reshape(-1)
    row_owner, col_owner = row // 2, col // 2
    row_at = (((row_owner % 2) ^ core) * 8 + row_owner // 2) * 2 + row % 2
    col_at = (((col_owner % 2) ^ xl) * 8 + (col_owner // 2 - z) % 8) * 2 + col % 2

    projected = (dot(var_embed, msg_weight) * col_coef[:, None]).astype(BF16)
    near = ring_gather(projected)
    far = ring_gather(swap(projected, "xl", 1))
    parts = near + [(16 + place, array) for place, array in far]
    (forward,) = tile_products(parts, col_at, row_at, hold(tiles, near[5][1]), 32, False)
    forward = forward.reshape(2, 8 * rows_here, H)
    scaled = (var_embed * col_coef[:, None]).astype(BF16)
    scaled = jnp.stack([scaled, swap(scaled, "xl", 1)])
    forward, scaled = lax.optimization_barrier((forward, scaled))
    sibling = swap(forward[1].astype(BF16), "c", 1)
    scaled, more = pair_start(scaled)
    partial = (forward[0] + sibling.astype(F32)).astype(BF16)
    partial = partial.reshape(8, rows_here, H)
    partial = lax.all_to_all(partial, ("xh", "y"), split_axis=0, concat_axis=0, tiled=True)
    frequency = jnp.exp(-math.log(10000.0) * jnp.arange(H // 2, dtype=F32) / (H // 2))
    phases = timestep[0].astype(F32) * frequency
    time_embed = jnp.concatenate([jnp.sin(phases), jnp.cos(phases)])
    base = dot(con_embed, self_weight) + time_embed[None, :]
    scale = jnp.broadcast_to(row_coef[:, None], con_embed.shape)
    partial, more, base, scale = lax.optimization_barrier((partial, more, base, scale))
    scaled = pair_end(scaled, *more)
    con_update, grad_pre, copies = mid(partial, base, scale, con_embed, cotangent)
    own = lax.all_to_all(copies, ("xh", "y"), split_axis=0, concat_axis=0, tiled=True)
    blocks = [block for _, _, block in scaled]
    own, blocks = lax.optimization_barrier((own, blocks))
    scaled = [(place, side, block) for (place, side, _), block in zip(scaled, blocks, strict=True)]
    own = own.reshape(8 * rows_here, H)
    other = swap(own, "c", 1)
    held = hold(tiles, own)
    grad_con = cotangent + dot(grad_pre, self_weight.T)
    local_self = dot(con_embed.T, grad_pre)
    backward, first = tile_products([(0, own), (16, other)], row_at, col_at, held, 32, True)
    backward = backward.reshape(2, 8, rows_here, H)
    local_msg = weight_partial(backward, scaled)
    grad_projected, grad_self, grad_msg = scatter_and_sum(backward, first, (local_self, local_msg))
    grad_lin = col_coef[:, None] * grad_projected
    grad_var = dot(grad_lin, msg_weight.T)
    return (con_update, grad_con, grad_var, grad_msg, grad_self)


def solution(mesh):
    fine = Mesh(np.asarray(mesh.devices).reshape(tuple(AXES.values())), tuple(AXES))
    cg, vg = ("z", "xl"), ("xh", "y", "c")
    in_specs = (
        P(cg + vg, None),
        P(vg + cg, None),
        P(cg + vg),
        P(vg + cg),
        P(),
        P(),
        P(),
        P(cg, vg, None),
        P(cg, vg, None),
        P(cg, vg, None, None, None),
        P(cg + vg, None),
    )
    out_specs = (P(cg + vg, None), P(cg + vg, None), P(vg + cg, None), P(), P())
    return jax.shard_map(body, mesh=fine, in_specs=in_specs, out_specs=out_specs, check_vma=False)
```

```python
import functools
import math

import jax
import jax.numpy as jnp
import numpy as np
from jax import lax
from jax.experimental import pallas as pl
from jax.experimental.pallas import tpu as pltpu
from jax.sharding import Mesh
from jax.sharding import PartitionSpec as P

H = 128
TB = 512
AXES = {"z": 8, "xl": 2, "xh": 2, "y": 4, "c": 2}
BF16 = jnp.bfloat16
F32 = jnp.float32


def shift(x, axis, by):
    n = AXES[axis]
    return lax.ppermute(x, axis, [(i, (i + by) % n) for i in range(n)])


def swap(x, axis, mask):
    return lax.ppermute(x, axis, [(i, i ^ mask) for i in range(AXES[axis])])


def ring_gather(x):
    half = x.shape[0] // 2
    parts = [(0, x)]
    up = down = x
    for step in (1, 2, 3):
        up, down = shift(up, "z", 1), shift(down, "z", -1)
        parts += [(2 * (8 - step), up), (2 * step, down)]
    parts += [(8, shift(up[:half], "z", 1)), (9, shift(down[half:], "z", -1))]
    return parts


def pair_start(x):
    up, down = shift(x, "z", 1), shift(x, "z", -1)
    more = shift(up, "z", 1), shift(down, "z", -1)
    return [(0, 0, x), (7, 0, up), (1, 0, down)], more


def pair_end(parts, up, down):
    parts = parts + [(6, 0, up), (2, 0, down)]
    up, down = shift(up, "z", 1), shift(down, "z", -1)
    parts += [(5, 0, up), (3, 0, down)]
    return parts + [(4, 0, shift(up[:1], "z", 1)), (4, 1, shift(down[1:], "z", -1))]


TREE = (("xl", 1), ("xh", 1), ("y", 1), ("y", 2), ("z", 1), ("z", 2), ("z", 4))


def slot_kernel(side, step, sums, up, down, *refs):
    outs, (block, sems) = refs[:-2], refs[-2:]
    if (side, step) != (1, 3):
        (mine, theirs), outs = outs[:2], outs[2:]
    steps = (step, 8 - step) if step else (0,)
    copies = [
        pltpu.make_async_copy(sums.at[side, p], block.at[i], sems.at[i])
        for i, p in enumerate(steps)
    ]
    for copy in copies:
        copy.start()
    if (side, step) != (1, 3):
        outs[-1][...] = mine[...] + theirs[...]
    for copy in copies:
        copy.wait()
    rows = block.shape[1]
    if step == 0:
        total = block[0] + up[...].astype(F32) + down[...].astype(F32)
        outs[0][...] = total.astype(outs[0].dtype)
    elif step == 3:
        half = rows // 2
        low, high = pl.ds(0, half), pl.ds(half, half)
        outs[0][low] = (block[0, low] + up[...].astype(F32)).astype(BF16)
        outs[0][high] = block[0, high].astype(BF16)
        outs[1][low] = block[1, low].astype(BF16)
        outs[1][high] = (block[1, high] + down[...].astype(F32)).astype(BF16)
    else:
        outs[0][...] = (block[0] + up[...].astype(F32)).astype(BF16)
        outs[1][...] = (block[1] + down[...].astype(F32)).astype(BF16)


def slot(sums, side, step, up, down, *tree):
    rows = sums.shape[2]
    if step:
        out = [jax.ShapeDtypeStruct((rows, H), BF16)] * 2
    else:
        out = [jax.ShapeDtypeStruct((rows, H), BF16 if side else F32)]
    out += [jax.ShapeDtypeStruct(x.shape, F32) for x in tree[:1]]
    return pl.pallas_call(
        functools.partial(slot_kernel, side, step),
        out_shape=tuple(out),
        in_specs=[ANY_SPEC] + [VMEM_SPEC] * (2 + len(tree)),
        out_specs=tuple([VMEM_SPEC] * len(out)),
        scratch_shapes=[pltpu.VMEM((2, rows, H), F32), pltpu.SemaphoreType.DMA((2,))],
        compiler_params=pltpu.CompilerParams(vmem_limit_bytes=8 << 20),
        cost_estimate=pl.CostEstimate(
            flops=2 * rows * H, bytes_accessed=8 * rows * H, transcendentals=0
        ),
        name="slot",
    )(sums, up, down, *tree)


def scatter_and_sum(sums, first, local_self, scaled):
    links, last = {}, {}
    for side in (1, 0):
        links[side] = shift(first[2 * side], "z", 1), shift(first[2 * side + 1], "z", -1)
    lead = lax.axis_index("c") == 0
    local_msg = weight_partial(sums, scaled)
    mine = jnp.where(lead, local_self, local_msg)
    mine = mine + swap(jnp.where(lead, local_msg, local_self), "c", 1)
    tree = iter(TREE)
    theirs = None
    for step in (3, 2, 1, 0):
        for side in (1, 0):
            if theirs is None:
                ends = slot(sums, side, step, *links[side])
            else:
                *ends, mine = slot(sums, side, step, *links[side], mine, theirs)
            if step:
                links[side] = shift(ends[0], "z", 1), shift(ends[1], "z", -1)
            else:
                last[side] = ends[0]
            if side or step:
                theirs = swap(mine, *next(tree))
    theirs = swap(mine, "c", 1)
    total = last[0] + swap(last[1], "xl", 1).astype(F32)
    return total, jnp.where(lead, mine, theirs), jnp.where(lead, theirs, mine)


GRANT = 24 << 20
HOLD_GRANT = 40 << 20
ANY_SPEC = pl.BlockSpec(memory_space=pl.ANY)
VMEM_SPEC = pl.BlockSpec(memory_space=pltpu.VMEM)


def hold_kernel(tiles, token, held, sem):
    copy = pltpu.make_async_copy(tiles, held, sem)
    copy.start()
    copy.wait()


def hold(tiles, token):
    return pl.pallas_call(
        hold_kernel,
        out_shape=jax.ShapeDtypeStruct(tiles.shape, tiles.dtype),
        in_specs=[ANY_SPEC, ANY_SPEC],
        out_specs=VMEM_SPEC,
        scratch_shapes=[pltpu.SemaphoreType.DMA],
        compiler_params=pltpu.CompilerParams(vmem_limit_bytes=HOLD_GRANT),
        cost_estimate=pl.CostEstimate(
            flops=0, bytes_accessed=4 * tiles.size, transcendentals=0
        ),
        name="hold_tiles",
    )(tiles, token)


def add_products(take, put, copies, source, held, total, transpose):
    for copy in copies:
        copy.start()

    def clear(k, carry):
        total[pl.ds(pl.multiple_of(k * TB, TB), TB), :] = jnp.zeros((TB, H), F32)
        return carry

    lax.fori_loop(0, total.shape[0] // TB, clear, 0)
    for copy in copies:
        copy.wait()

    def multiply(k, carry):
        rows = source[pl.ds(pl.multiple_of(take[k] * TB, TB), TB), :]
        target = pl.multiple_of(put[k] * TB, TB)
        width = TB // 2
        for part in range(2):
            cut = pl.ds(part * width, width)
            if transpose:
                product = lax.dot_general(
                    held[k, :, cut], rows, (((0,), (0,)), ((), ())), preferred_element_type=F32
                )
            else:
                product = jnp.dot(held[k, cut, :], rows, preferred_element_type=F32)
            at = pl.ds(pl.multiple_of(target + part * width, width), width)
            total[at, :] += product
        return carry

    lax.fori_loop(0, held.shape[0], multiply, 0)


def tile_kernel(places, transpose, take, put, *refs):
    n = len(places)
    sources, held, outs, (source, sems) = refs[:n], refs[n], refs[n + 1 : -2], refs[-2:]
    total = outs[0]
    copies = [
        pltpu.make_async_copy(ref, source.at[pl.ds(place * TB, ref.shape[0])], sems.at[i])
        for i, (place, ref) in enumerate(zip(places, sources, strict=True))
    ]
    add_products(take, put, copies, source, held, total, transpose)
    for i, first in enumerate(outs[1:]):
        half = first.shape[0]
        first[...] = total[pl.ds((i // 2 * 8 + 4) * 2 * half + i % 2 * half, half), :].astype(BF16)


def tile_products(parts, take, put, held, blocks, transpose):
    arrays = [array for _, array in parts]
    out = [jax.ShapeDtypeStruct((blocks * TB, H), F32)]
    if transpose:
        out += [jax.ShapeDtypeStruct((blocks * TB // 32, H), BF16)] * 4
    return pl.pallas_call(
        functools.partial(tile_kernel, tuple(place for place, _ in parts), transpose),
        out_shape=tuple(out),
        grid_spec=pltpu.PrefetchScalarGridSpec(
            num_scalar_prefetch=2,
            grid=(),
            in_specs=[ANY_SPEC] * len(arrays) + [VMEM_SPEC],
            out_specs=tuple([VMEM_SPEC] * len(out)),
            scratch_shapes=[
                pltpu.VMEM((blocks * TB, H), BF16),
                pltpu.SemaphoreType.DMA((len(arrays),)),
            ],
        ),
        compiler_params=pltpu.CompilerParams(vmem_limit_bytes=GRANT),
        cost_estimate=pl.CostEstimate(
            flops=2 * held.size * H, bytes_accessed=2 * held.size + blocks * TB * H * 6, transcendentals=0
        ),
        name="tiles_back" if transpose else "tiles_forward",
    )(take, put, *arrays, held)


def weight_kernel(places, sums, *refs):
    n = len(places)
    scaled, (out,) = refs[:n], refs[n:]
    out[...] = jnp.zeros_like(out)
    for (place, side), ref in zip(places, scaled, strict=True):
        for i in range(ref.shape[0]):
            block = sums[side + i, place]
            high = block.astype(BF16)
            low = (block - high.astype(F32)).astype(BF16)
            both = lax.dot_general(
                ref[i],
                jnp.concatenate([high, low], axis=1),
                (((0,), (0,)), ((), ())),
                preferred_element_type=F32,
            )
            out[...] += both[:, :H] + both[:, H:]


def weight_partial(sums, scaled):
    arrays = [array for _, _, array in scaled]
    return pl.pallas_call(
        functools.partial(weight_kernel, tuple((place, side) for place, side, _ in scaled)),
        out_shape=jax.ShapeDtypeStruct((H, H), F32),
        in_specs=[VMEM_SPEC] * (1 + len(arrays)),
        out_specs=VMEM_SPEC,
        compiler_params=pltpu.CompilerParams(vmem_limit_bytes=GRANT),
        cost_estimate=pl.CostEstimate(
            flops=4 * sums.size * H, bytes_accessed=6 * sums.size, transcendentals=0
        ),
        name="weight_partial",
    )(sums, *arrays)


def mid_kernel(partial, base, scale, con, cot, update, pre, copies, con_in, cot_in, sent, in_sems, out_sems):
    parts = in_sems.shape[1]
    width = con_in.shape[0] // parts

    def cut(k):
        return pl.ds(pl.multiple_of(k * width, width), width)

    def load(k, i, ref, held):
        return pltpu.make_async_copy(ref.at[cut(k)], held.at[cut(k)], in_sems.at[i, k])

    def send(k, i):
        return pltpu.make_async_copy(sent.at[cut(k)], copies.at[i, cut(k)], out_sems.at[i, k])

    for k in range(parts):
        load(k, 0, con, con_in).start()
        load(k, 1, cot, cot_in).start()

    def step(k, carry):
        at = cut(k)
        messages = partial[0, at, :].astype(F32)
        for i in range(1, partial.shape[0]):
            messages += partial[i, at, :].astype(F32)
        preact = base[at, :] + scale[at, :] * messages
        gate = jax.nn.sigmoid(preact)
        load(k, 0, con, con_in).wait()
        load(k, 1, cot, cot_in).wait()
        update[at, :] = con_in[at, :] + preact * gate
        grad = cot_in[at, :] * gate * (1.0 + preact * (1.0 - gate))
        pre[at, :] = grad
        sent[at, :] = (scale[at, :] * grad).astype(BF16)
        for i in range(copies.shape[0]):
            send(k, i).start()
        return carry

    lax.fori_loop(0, parts, step, 0)
    for k in range(parts):
        for i in range(copies.shape[0]):
            send(k, i).wait()


def mid(partial, base, scale, con, cot):
    parts = 4
    return pl.pallas_call(
        mid_kernel,
        out_shape=(
            jax.ShapeDtypeStruct(con.shape, F32),
            jax.ShapeDtypeStruct(con.shape, F32),
            jax.ShapeDtypeStruct(partial.shape, BF16),
        ),
        in_specs=[VMEM_SPEC] * 3 + [pl.BlockSpec(memory_space=pltpu.HBM)] * 2,
        out_specs=(VMEM_SPEC, VMEM_SPEC, pl.BlockSpec(memory_space=pltpu.HBM)),
        scratch_shapes=[
            pltpu.VMEM(con.shape, F32),
            pltpu.VMEM(con.shape, F32),
            pltpu.VMEM(con.shape, BF16),
            pltpu.SemaphoreType.DMA((2, parts)),
            pltpu.SemaphoreType.DMA((partial.shape[0], parts)),
        ],
        compiler_params=pltpu.CompilerParams(vmem_limit_bytes=12 << 20),
        cost_estimate=pl.CostEstimate(
            flops=24 * con.size, bytes_accessed=56 * con.size, transcendentals=con.size
        ),
        name="mid",
    )(partial, base, scale, con, cot)


def body(
    con_embed,
    var_embed,
    row_coef,
    col_coef,
    self_weight,
    msg_weight,
    timestep,
    tile_rows,
    tile_cols,
    pattern,
    cotangent,
):
    dot = functools.partial(
        jnp.dot, precision=lax.Precision.HIGHEST, preferred_element_type=F32
    )
    rows_here = con_embed.shape[0]
    z, xl, core = lax.axis_index("z"), lax.axis_index("xl"), lax.axis_index("c")
    tiles = pattern.reshape(-1, TB, TB)
    row, col = tile_rows.reshape(-1), tile_cols.reshape(-1)
    row_owner, col_owner = row // 2, col // 2
    row_at = (((row_owner % 2) ^ core) * 8 + row_owner // 2) * 2 + row % 2
    col_at = (((col_owner % 2) ^ xl) * 8 + (col_owner // 2 - z) % 8) * 2 + col % 2

    projected = (dot(var_embed, msg_weight) * col_coef[:, None]).astype(BF16)
    near = ring_gather(projected)
    far = ring_gather(swap(projected, "xl", 1))
    parts = near + [(16 + place, array) for place, array in far]
    (forward,) = tile_products(parts, col_at, row_at, hold(tiles, near[5][1]), 32, False)
    forward = forward.reshape(2, 8 * rows_here, H)
    scaled = (var_embed * col_coef[:, None]).astype(BF16)
    scaled = jnp.stack([scaled, swap(scaled, "xl", 1)])
    forward, scaled = lax.optimization_barrier((forward, scaled))
    sibling = swap(forward[1].astype(BF16), "c", 1)
    scaled, more = pair_start(scaled)
    partial = (forward[0] + sibling.astype(F32)).astype(BF16)
    partial = partial.reshape(8, rows_here, H)
    partial = lax.all_to_all(partial, ("xh", "y"), split_axis=0, concat_axis=0, tiled=True)
    frequency = jnp.exp(-math.log(10000.0) * jnp.arange(H // 2, dtype=F32) / (H // 2))
    phases = timestep[0].astype(F32) * frequency
    time_embed = jnp.concatenate([jnp.sin(phases), jnp.cos(phases)])
    base = dot(con_embed, self_weight) + time_embed[None, :]
    scale = jnp.broadcast_to(row_coef[:, None], con_embed.shape)
    partial, more, base, scale = lax.optimization_barrier((partial, more, base, scale))
    scaled = pair_end(scaled, *more)
    con_update, grad_pre, copies = mid(partial, base, scale, con_embed, cotangent)
    own = lax.all_to_all(copies, ("xh", "y"), split_axis=0, concat_axis=0, tiled=True)
    blocks = [block for _, _, block in scaled]
    own, blocks = lax.optimization_barrier((own, blocks))
    scaled = [(place, side, block) for (place, side, _), block in zip(scaled, blocks, strict=True)]
    own = own.reshape(8 * rows_here, H)
    other = swap(own, "c", 1)
    held = hold(tiles, own)
    grad_con = cotangent + dot(grad_pre, self_weight.T)
    local_self = dot(con_embed.T, grad_pre)
    backward, *first = tile_products([(0, own), (16, other)], row_at, col_at, held, 32, True)
    backward = backward.reshape(2, 8, rows_here, H)
    grad_projected, grad_self, grad_msg = scatter_and_sum(backward, first, local_self, scaled)
    grad_lin = col_coef[:, None] * grad_projected
    grad_var = dot(grad_lin, msg_weight.T)
    return (con_update, grad_con, grad_var, grad_msg, grad_self)


def solution(mesh):
    fine = Mesh(np.asarray(mesh.devices).reshape(tuple(AXES.values())), tuple(AXES))
    cg, vg = ("z", "xl"), ("xh", "y", "c")
    in_specs = (
        P(cg + vg, None),
        P(vg + cg, None),
        P(cg + vg),
        P(vg + cg),
        P(),
        P(),
        P(),
        P(cg, vg, None),
        P(cg, vg, None),
        P(cg, vg, None, None, None),
        P(cg + vg, None),
    )
    out_specs = (P(cg + vg, None), P(cg + vg, None), P(vg + cg, None), P(), P())
    return jax.shard_map(body, mesh=fine, in_specs=in_specs, out_specs=out_specs, check_vma=False)
```

```python
import functools
import math

import jax
import jax.numpy as jnp
import numpy as np
from jax import lax
from jax.experimental import pallas as pl
from jax.experimental.pallas import tpu as pltpu
from jax.sharding import Mesh
from jax.sharding import PartitionSpec as P

H = 128
TB = 512
AXES = {"z": 8, "xl": 2, "xh": 2, "y": 4, "c": 2}
BF16 = jnp.bfloat16
F32 = jnp.float32


def shift(x, axis, by):
    n = AXES[axis]
    return lax.ppermute(x, axis, [(i, (i + by) % n) for i in range(n)])


def swap(x, axis, mask):
    return lax.ppermute(x, axis, [(i, i ^ mask) for i in range(AXES[axis])])


def ring_gather(x):
    half = x.shape[0] // 2
    parts = [(0, x)]
    up = down = x
    for step in (1, 2, 3):
        up, down = shift(up, "z", 1), shift(down, "z", -1)
        parts += [(2 * (8 - step), up), (2 * step, down)]
    parts += [(8, shift(up[:half], "z", 1)), (9, shift(down[half:], "z", -1))]
    return parts


def pair_start(x):
    up, down = shift(x, "z", 1), shift(x, "z", -1)
    more = shift(up, "z", 1), shift(down, "z", -1)
    return [(0, 0, x), (7, 0, up), (1, 0, down)], more


def pair_end(parts, up, down):
    parts = parts + [(6, 0, up), (2, 0, down)]
    up, down = shift(up, "z", 1), shift(down, "z", -1)
    parts += [(5, 0, up), (3, 0, down)]
    return parts + [(4, 0, shift(up[:1], "z", 1)), (4, 1, shift(down[1:], "z", -1))]


TREE = (("c", 1), ("xl", 1), ("xh", 1), ("y", 1), ("y", 2), ("z", 1), ("z", 2), ("z", 4))


def slot_kernel(side, step, sums, up, down, *refs):
    outs, (block, sems) = refs[:-2], refs[-2:]
    if (side, step) != (1, 3):
        (mine, theirs), outs = outs[:2], outs[2:]
    steps = (step, 8 - step) if step else (0,)
    copies = [
        pltpu.make_async_copy(sums.at[side, p], block.at[i], sems.at[i])
        for i, p in enumerate(steps)
    ]
    for copy in copies:
        copy.start()
    if (side, step) != (1, 3):
        outs[-1][...] = mine[...] + theirs[...]
    for copy in copies:
        copy.wait()
    rows = block.shape[1]
    if step == 0:
        total = block[0] + up[...].astype(F32) + down[...].astype(F32)
        outs[0][...] = total.astype(outs[0].dtype)
    elif step == 3:
        half = rows // 2
        low, high = pl.ds(0, half), pl.ds(half, half)
        outs[0][low] = (block[0, low] + up[side].astype(F32)).astype(BF16)
        outs[0][high] = block[0, high].astype(BF16)
        outs[1][low] = block[1, low].astype(BF16)
        outs[1][high] = (block[1, high] + down[side].astype(F32)).astype(BF16)
    else:
        outs[0][...] = (block[0] + up[...].astype(F32)).astype(BF16)
        outs[1][...] = (block[1] + down[...].astype(F32)).astype(BF16)


def slot(sums, side, step, up, down, *tree):
    rows = sums.shape[2]
    if step:
        out = [jax.ShapeDtypeStruct((rows, H), BF16)] * 2
    else:
        out = [jax.ShapeDtypeStruct((rows, H), BF16 if side else F32)]
    out += [jax.ShapeDtypeStruct(x.shape, F32) for x in tree[:1]]
    return pl.pallas_call(
        functools.partial(slot_kernel, side, step),
        out_shape=tuple(out),
        in_specs=[ANY_SPEC] + [VMEM_SPEC] * (2 + len(tree)),
        out_specs=tuple([VMEM_SPEC] * len(out)),
        scratch_shapes=[pltpu.VMEM((2, rows, H), F32), pltpu.SemaphoreType.DMA((2,))],
        compiler_params=pltpu.CompilerParams(vmem_limit_bytes=8 << 20),
        cost_estimate=pl.CostEstimate(
            flops=2 * rows * H, bytes_accessed=8 * rows * H, transcendentals=0
        ),
        name="slot",
    )(sums, up, down, *tree)


def scatter_and_sum(sums, first, weights):
    links = dict.fromkeys((1, 0), (shift(first[0], "z", 1), shift(first[1], "z", -1)))
    last = {}
    tree = iter(TREE)
    theirs = None
    for step in (3, 2, 1, 0):
        for side in (1, 0):
            if theirs is None:
                ends = slot(sums, side, step, *links[side])
            else:
                *ends, weights = slot(sums, side, step, *links[side], weights, theirs)
            if step:
                links[side] = shift(ends[0], "z", 1), shift(ends[1], "z", -1)
            else:
                last[side] = ends[0]
            theirs = swap(weights, *next(tree))
    return last[0] + swap(last[1], "xl", 1).astype(F32), weights + theirs


GRANT = 24 << 20
HOLD_GRANT = 40 << 20
ANY_SPEC = pl.BlockSpec(memory_space=pl.ANY)
VMEM_SPEC = pl.BlockSpec(memory_space=pltpu.VMEM)


def hold_kernel(tiles, token, held, sem):
    copy = pltpu.make_async_copy(tiles, held, sem)
    copy.start()
    copy.wait()


def hold(tiles, token):
    return pl.pallas_call(
        hold_kernel,
        out_shape=jax.ShapeDtypeStruct(tiles.shape, tiles.dtype),
        in_specs=[ANY_SPEC, ANY_SPEC],
        out_specs=VMEM_SPEC,
        scratch_shapes=[pltpu.SemaphoreType.DMA],
        compiler_params=pltpu.CompilerParams(vmem_limit_bytes=HOLD_GRANT),
        cost_estimate=pl.CostEstimate(
            flops=0, bytes_accessed=4 * tiles.size, transcendentals=0
        ),
        name="hold_tiles",
    )(tiles, token)


def add_products(take, put, copies, source, held, total, transpose):
    for copy in copies:
        copy.start()

    def clear(k, carry):
        total[pl.ds(pl.multiple_of(k * TB, TB), TB), :] = jnp.zeros((TB, H), F32)
        return carry

    lax.fori_loop(0, total.shape[0] // TB, clear, 0)
    for copy in copies:
        copy.wait()

    def multiply(k, carry):
        rows = source[pl.ds(pl.multiple_of(take[k] * TB, TB), TB), :]
        target = pl.multiple_of(put[k] * TB, TB)
        width = TB // 2
        for part in range(2):
            cut = pl.ds(part * width, width)
            if transpose:
                product = lax.dot_general(
                    held[k, :, cut], rows, (((0,), (0,)), ((), ())), preferred_element_type=F32
                )
            else:
                product = jnp.dot(held[k, cut, :], rows, preferred_element_type=F32)
            at = pl.ds(pl.multiple_of(target + part * width, width), width)
            total[at, :] += product
        return carry

    lax.fori_loop(0, held.shape[0], multiply, 0)


def tile_kernel(places, transpose, take, put, *refs):
    n = len(places)
    sources, held, outs, (source, sems) = refs[:n], refs[n], refs[n + 1 : -2], refs[-2:]
    total = outs[0]
    copies = [
        pltpu.make_async_copy(ref, source.at[pl.ds(place * TB, ref.shape[0])], sems.at[i])
        for i, (place, ref) in enumerate(zip(places, sources, strict=True))
    ]
    add_products(take, put, copies, source, held, total, transpose)
    for i, first in enumerate(outs[1:]):
        half = first.shape[1]
        for side in range(2):
            first[side] = total[pl.ds(((side * 8 + 4) * 2 + i) * half, half), :].astype(BF16)


def tile_products(parts, take, put, held, blocks, transpose):
    arrays = [array for _, array in parts]
    out = [jax.ShapeDtypeStruct((blocks * TB, H), F32)]
    if transpose:
        out += [jax.ShapeDtypeStruct((2, blocks * TB // 32, H), BF16)] * 2
    return pl.pallas_call(
        functools.partial(tile_kernel, tuple(place for place, _ in parts), transpose),
        out_shape=tuple(out),
        grid_spec=pltpu.PrefetchScalarGridSpec(
            num_scalar_prefetch=2,
            grid=(),
            in_specs=[ANY_SPEC] * len(arrays) + [VMEM_SPEC],
            out_specs=tuple([VMEM_SPEC] * len(out)),
            scratch_shapes=[
                pltpu.VMEM((blocks * TB, H), BF16),
                pltpu.SemaphoreType.DMA((len(arrays),)),
            ],
        ),
        compiler_params=pltpu.CompilerParams(vmem_limit_bytes=GRANT),
        cost_estimate=pl.CostEstimate(
            flops=2 * held.size * H, bytes_accessed=2 * held.size + blocks * TB * H * 6, transcendentals=0
        ),
        name="tiles_back" if transpose else "tiles_forward",
    )(take, put, *arrays, held)


def weight_kernel(places, sums, *refs):
    n = len(places)
    scaled, (out,) = refs[:n], refs[n:]
    out[...] = jnp.zeros_like(out)
    for (place, side), ref in zip(places, scaled, strict=True):
        for i in range(ref.shape[0]):
            block = sums[side + i, place]
            high = block.astype(BF16)
            low = (block - high.astype(F32)).astype(BF16)
            both = lax.dot_general(
                ref[i],
                jnp.concatenate([high, low], axis=1),
                (((0,), (0,)), ((), ())),
                preferred_element_type=F32,
            )
            out[...] += both[:, :H] + both[:, H:]


def weight_partial(sums, scaled):
    arrays = [array for _, _, array in scaled]
    return pl.pallas_call(
        functools.partial(weight_kernel, tuple((place, side) for place, side, _ in scaled)),
        out_shape=jax.ShapeDtypeStruct((H, H), F32),
        in_specs=[VMEM_SPEC] * (1 + len(arrays)),
        out_specs=VMEM_SPEC,
        compiler_params=pltpu.CompilerParams(vmem_limit_bytes=GRANT),
        cost_estimate=pl.CostEstimate(
            flops=4 * sums.size * H, bytes_accessed=6 * sums.size, transcendentals=0
        ),
        name="weight_partial",
    )(sums, *arrays)


def mid_kernel(partial, base, scale, con, cot, update, pre, copies):
    width = 128

    def step(k, carry):
        at = pl.ds(pl.multiple_of(k * width, width), width)
        messages = partial[0, at, :].astype(F32)
        for i in range(1, partial.shape[0]):
            messages += partial[i, at, :].astype(F32)
        preact = base[at, :] + scale[at, :] * messages
        gate = jax.nn.sigmoid(preact)
        update[at, :] = con[at, :] + preact * gate
        grad = cot[at, :] * gate * (1.0 + preact * (1.0 - gate))
        pre[at, :] = grad
        sent = (scale[at, :] * grad).astype(BF16)
        for i in range(copies.shape[0]):
            copies[i, at, :] = sent
        return carry

    lax.fori_loop(0, con.shape[0] // width, step, 0)


def mid(partial, base, scale, con, cot):
    return pl.pallas_call(
        mid_kernel,
        out_shape=(
            jax.ShapeDtypeStruct(con.shape, F32),
            jax.ShapeDtypeStruct(con.shape, F32),
            jax.ShapeDtypeStruct(partial.shape, BF16),
        ),
        in_specs=[VMEM_SPEC] * 5,
        out_specs=(VMEM_SPEC,) * 3,
        compiler_params=pltpu.CompilerParams(vmem_limit_bytes=12 << 20),
        cost_estimate=pl.CostEstimate(
            flops=24 * con.size, bytes_accessed=56 * con.size, transcendentals=con.size
        ),
        name="mid",
    )(partial, base, scale, con, cot)


def body(
    con_embed,
    var_embed,
    row_coef,
    col_coef,
    self_weight,
    msg_weight,
    timestep,
    tile_rows,
    tile_cols,
    pattern,
    cotangent,
):
    dot = functools.partial(
        jnp.dot, precision=lax.Precision.HIGHEST, preferred_element_type=F32
    )
    rows_here = con_embed.shape[0]
    z, xl, core = lax.axis_index("z"), lax.axis_index("xl"), lax.axis_index("c")
    tiles = pattern.reshape(-1, TB, TB)
    row, col = tile_rows.reshape(-1), tile_cols.reshape(-1)
    row_owner, col_owner = row // 2, col // 2
    row_at = (((row_owner % 2) ^ core) * 8 + row_owner // 2) * 2 + row % 2
    col_at = (((col_owner % 2) ^ xl) * 8 + (col_owner // 2 - z) % 8) * 2 + col % 2

    projected = (dot(var_embed, msg_weight) * col_coef[:, None]).astype(BF16)
    near = ring_gather(projected)
    far = ring_gather(swap(projected, "xl", 1))
    parts = near + [(16 + place, array) for place, array in far]
    (forward,) = tile_products(parts, col_at, row_at, hold(tiles, near[5][1]), 32, False)
    forward = forward.reshape(2, 8 * rows_here, H)
    scaled = (var_embed * col_coef[:, None]).astype(BF16)
    scaled = jnp.stack([scaled, swap(scaled, "xl", 1)])
    forward, scaled = lax.optimization_barrier((forward, scaled))
    sibling = swap(forward[1].astype(BF16), "c", 1)
    scaled, more = pair_start(scaled)
    partial = (forward[0] + sibling.astype(F32)).astype(BF16)
    partial = partial.reshape(8, rows_here, H)
    partial = lax.all_to_all(partial, ("xh", "y"), split_axis=0, concat_axis=0, tiled=True)
    frequency = jnp.exp(-math.log(10000.0) * jnp.arange(H // 2, dtype=F32) / (H // 2))
    phases = timestep[0].astype(F32) * frequency
    time_embed = jnp.concatenate([jnp.sin(phases), jnp.cos(phases)])
    base = dot(con_embed, self_weight) + time_embed[None, :]
    scale = jnp.broadcast_to(row_coef[:, None], con_embed.shape)
    partial, more, base, scale = lax.optimization_barrier((partial, more, base, scale))
    scaled = pair_end(scaled, *more)
    con_update, grad_pre, copies = mid(partial, base, scale, con_embed, cotangent)
    own = lax.all_to_all(copies, ("xh", "y"), split_axis=0, concat_axis=0, tiled=True)
    blocks = [block for _, _, block in scaled]
    own, blocks = lax.optimization_barrier((own, blocks))
    scaled = [(place, side, block) for (place, side, _), block in zip(scaled, blocks, strict=True)]
    own = own.reshape(8 * rows_here, H)
    other = swap(own, "c", 1)
    held = hold(tiles, own)
    grad_con = cotangent + dot(grad_pre, self_weight.T)
    local_self = dot(con_embed.T, grad_pre)
    backward, *first = tile_products([(0, own), (16, other)], row_at, col_at, held, 32, True)
    backward = backward.reshape(2, 8, rows_here, H)
    local_msg = weight_partial(backward, scaled)
    grad_projected, weights = scatter_and_sum(backward, first, jnp.stack([local_self, local_msg]))
    grad_lin = col_coef[:, None] * grad_projected
    grad_var = dot(grad_lin, msg_weight.T)
    return (con_update, grad_con, grad_var, weights[1], weights[0])


def solution(mesh):
    fine = Mesh(np.asarray(mesh.devices).reshape(tuple(AXES.values())), tuple(AXES))
    cg, vg = ("z", "xl"), ("xh", "y", "c")
    in_specs = (
        P(cg + vg, None),
        P(vg + cg, None),
        P(cg + vg),
        P(vg + cg),
        P(),
        P(),
        P(),
        P(cg, vg, None),
        P(cg, vg, None),
        P(cg, vg, None, None, None),
        P(cg + vg, None),
    )
    out_specs = (P(cg + vg, None), P(cg + vg, None), P(vg + cg, None), P(), P())
    return jax.shard_map(body, mesh=fine, in_specs=in_specs, out_specs=out_specs, check_vma=False)
```

```python
import functools
import math

import jax
import jax.numpy as jnp
import numpy as np
from jax import lax
from jax.experimental import pallas as pl
from jax.experimental.pallas import tpu as pltpu
from jax.sharding import Mesh
from jax.sharding import PartitionSpec as P

H = 128
TB = 512
AXES = {"z": 8, "xl": 2, "xh": 2, "y": 4, "c": 2}
BF16 = jnp.bfloat16
F32 = jnp.float32


def shift(x, axis, by):
    n = AXES[axis]
    return lax.ppermute(x, axis, [(i, (i + by) % n) for i in range(n)])


def swap(x, axis, mask):
    return lax.ppermute(x, axis, [(i, i ^ mask) for i in range(AXES[axis])])


def ring_gather(x):
    half = x.shape[0] // 2
    parts = [(0, x)]
    up = down = x
    for step in (1, 2, 3):
        up, down = shift(up, "z", 1), shift(down, "z", -1)
        parts += [(2 * (8 - step), up), (2 * step, down)]
    parts += [(8, shift(up[:half], "z", 1)), (9, shift(down[half:], "z", -1))]
    return parts


def pair_start(x):
    up, down = shift(x, "z", 1), shift(x, "z", -1)
    more = shift(up, "z", 1), shift(down, "z", -1)
    return [(0, 0, x), (7, 0, up), (1, 0, down)], more


def pair_end(parts, up, down):
    parts = parts + [(6, 0, up), (2, 0, down)]
    up, down = shift(up, "z", 1), shift(down, "z", -1)
    parts += [(5, 0, up), (3, 0, down)]
    return parts + [(4, 0, shift(up[:1], "z", 1)), (4, 1, shift(down[1:], "z", -1))]


TREE = (("xl", 1), ("xh", 1), ("y", 1), ("y", 2), ("z", 1), ("z", 2), ("z", 4), ("c", 1))


def slot_kernel(side, step, sums, up, down, *refs):
    outs, (block, sems) = refs[:-2], refs[-2:]
    if (side, step) != (1, 3):
        (mine, theirs), outs = outs[:2], outs[2:]
    steps = (step, 8 - step) if step else (0,)
    copies = [
        pltpu.make_async_copy(sums.at[side, p], block.at[i], sems.at[i])
        for i, p in enumerate(steps)
    ]
    for copy in copies:
        copy.start()
    if (side, step) != (1, 3):
        outs[-1][...] = mine[...] + theirs[...]
    for copy in copies:
        copy.wait()
    rows = block.shape[1]
    half, width = rows // 2, 64

    def each(begin, end, action):
        def body(k, carry):
            action(pl.multiple_of(begin + k * width, width))
            return carry

        lax.fori_loop(0, (end - begin) // width, body, 0)

    def add(i, ref, skip=0):
        def action(at):
            here = pl.ds(at, width)
            outs[i][here] = (block[i, here] + ref[pl.ds(at - skip, width)].astype(F32)).astype(BF16)

        return action

    def keep(i):
        def action(at):
            here = pl.ds(at, width)
            outs[i][here] = block[i, here].astype(BF16)

        return action

    def finish(at):
        here = pl.ds(at, width)
        total = block[0, here] + up[here].astype(F32) + down[here].astype(F32)
        outs[0][here] = total.astype(outs[0].dtype)

    if step == 0:
        each(0, rows, finish)
    elif step == 3:
        each(0, half, add(0, up.at[side]))
        each(half, rows, keep(0))
        each(0, half, keep(1))
        each(half, rows, add(1, down.at[side], half))
    else:
        each(0, rows, add(0, up))
        each(0, rows, add(1, down))


def slot(sums, side, step, up, down, *tree):
    rows = sums.shape[2]
    if step:
        out = [jax.ShapeDtypeStruct((rows, H), BF16)] * 2
    else:
        out = [jax.ShapeDtypeStruct((rows, H), BF16 if side else F32)]
    out += [jax.ShapeDtypeStruct(x.shape, F32) for x in tree[:1]]
    return pl.pallas_call(
        functools.partial(slot_kernel, side, step),
        out_shape=tuple(out),
        in_specs=[ANY_SPEC] + [VMEM_SPEC] * (2 + len(tree)),
        out_specs=tuple([VMEM_SPEC] * len(out)),
        scratch_shapes=[pltpu.VMEM((2, rows, H), F32), pltpu.SemaphoreType.DMA((2,))],
        compiler_params=pltpu.CompilerParams(vmem_limit_bytes=8 << 20),
        cost_estimate=pl.CostEstimate(
            flops=2 * rows * H, bytes_accessed=8 * rows * H, transcendentals=0
        ),
        name="slot",
    )(sums, up, down, *tree)


def scatter_and_sum(sums, first, weights):
    links = dict.fromkeys((1, 0), (shift(first[0], "z", 1), shift(first[1], "z", -1)))
    last = {}
    tree = iter(TREE)
    theirs = None
    for step in (3, 2, 1, 0):
        for side in (1, 0):
            if theirs is None:
                ends = slot(sums, side, step, *links[side])
            else:
                *ends, weights = slot(sums, side, step, *links[side], weights, theirs)
            if step:
                links[side] = shift(ends[0], "z", 1), shift(ends[1], "z", -1)
            else:
                last[side] = ends[0]
            theirs = swap(weights, *next(tree))
    return last[0] + swap(last[1], "xl", 1).astype(F32), weights + theirs


GRANT = 24 << 20
HOLD_GRANT = 40 << 20
ANY_SPEC = pl.BlockSpec(memory_space=pl.ANY)
VMEM_SPEC = pl.BlockSpec(memory_space=pltpu.VMEM)


def hold_kernel(tiles, token, held, sem):
    copy = pltpu.make_async_copy(tiles, held, sem)
    copy.start()
    copy.wait()


def hold(tiles, token):
    return pl.pallas_call(
        hold_kernel,
        out_shape=jax.ShapeDtypeStruct(tiles.shape, tiles.dtype),
        in_specs=[ANY_SPEC, ANY_SPEC],
        out_specs=VMEM_SPEC,
        scratch_shapes=[pltpu.SemaphoreType.DMA],
        compiler_params=pltpu.CompilerParams(vmem_limit_bytes=HOLD_GRANT),
        cost_estimate=pl.CostEstimate(
            flops=0, bytes_accessed=4 * tiles.size, transcendentals=0
        ),
        name="hold_tiles",
    )(tiles, token)


def add_products(take, put, copies, source, held, total, transpose):
    for copy in copies:
        copy.start()

    def clear(k, carry):
        total[pl.ds(pl.multiple_of(k * TB, TB), TB), :] = jnp.zeros((TB, H), F32)
        return carry

    lax.fori_loop(0, total.shape[0] // TB, clear, 0)
    for copy in copies:
        copy.wait()

    def multiply(k, carry):
        rows = source[pl.ds(pl.multiple_of(take[k] * TB, TB), TB), :]
        target = pl.multiple_of(put[k] * TB, TB)
        width = TB // 2
        for part in range(2):
            cut = pl.ds(part * width, width)
            if transpose:
                product = lax.dot_general(
                    held[k, :, cut], rows, (((0,), (0,)), ((), ())), preferred_element_type=F32
                )
            else:
                product = jnp.dot(held[k, cut, :], rows, preferred_element_type=F32)
            at = pl.ds(pl.multiple_of(target + part * width, width), width)
            total[at, :] += product
        return carry

    lax.fori_loop(0, held.shape[0], multiply, 0)


def tile_kernel(places, transpose, take, put, *refs):
    n = len(places)
    sources, held, outs, (source, sems) = refs[:n], refs[n], refs[n + 1 : -2], refs[-2:]
    total = outs[0]
    copies = [
        pltpu.make_async_copy(ref, source.at[pl.ds(place * TB, ref.shape[0])], sems.at[i])
        for i, (place, ref) in enumerate(zip(places, sources, strict=True))
    ]
    add_products(take, put, copies, source, held, total, transpose)
    for i, first in enumerate(outs[1:]):
        half = first.shape[1]
        for side in range(2):
            first[side] = total[pl.ds(((side * 8 + 4) * 2 + i) * half, half), :].astype(BF16)


def tile_products(parts, take, put, held, blocks, transpose):
    arrays = [array for _, array in parts]
    out = [jax.ShapeDtypeStruct((blocks * TB, H), F32)]
    if transpose:
        out += [jax.ShapeDtypeStruct((2, blocks * TB // 32, H), BF16)] * 2
    return pl.pallas_call(
        functools.partial(tile_kernel, tuple(place for place, _ in parts), transpose),
        out_shape=tuple(out),
        grid_spec=pltpu.PrefetchScalarGridSpec(
            num_scalar_prefetch=2,
            grid=(),
            in_specs=[ANY_SPEC] * len(arrays) + [VMEM_SPEC],
            out_specs=tuple([VMEM_SPEC] * len(out)),
            scratch_shapes=[
                pltpu.VMEM((blocks * TB, H), BF16),
                pltpu.SemaphoreType.DMA((len(arrays),)),
            ],
        ),
        compiler_params=pltpu.CompilerParams(vmem_limit_bytes=GRANT),
        cost_estimate=pl.CostEstimate(
            flops=2 * held.size * H, bytes_accessed=2 * held.size + blocks * TB * H * 6, transcendentals=0
        ),
        name="tiles_back" if transpose else "tiles_forward",
    )(take, put, *arrays, held)


def weight_kernel(places, sums, *refs):
    n = len(places)
    scaled, (out,) = refs[:n], refs[n:]
    out[...] = jnp.zeros_like(out)
    width = 256
    for (place, side), ref in zip(places, scaled, strict=True):
        pieces = ref.shape[1] // width

        def step(k, total, ref=ref, place=place, side=side, pieces=pieces):
            i, at = k // pieces, pl.ds(pl.multiple_of(k % pieces * width, width), width)
            block = sums[side + i, place, at]
            high = block.astype(BF16)
            low = (block - high.astype(F32)).astype(BF16)
            both = lax.dot_general(
                ref[i, at],
                jnp.concatenate([high, low], axis=1),
                (((0,), (0,)), ((), ())),
                preferred_element_type=F32,
            )
            return total + both[:, :H] + both[:, H:]

        out[...] += lax.fori_loop(0, ref.shape[0] * pieces, step, jnp.zeros(out.shape, F32))


def weight_partial(sums, scaled):
    arrays = [array for _, _, array in scaled]
    return pl.pallas_call(
        functools.partial(weight_kernel, tuple((place, side) for place, side, _ in scaled)),
        out_shape=jax.ShapeDtypeStruct((H, H), F32),
        in_specs=[VMEM_SPEC] * (1 + len(arrays)),
        out_specs=VMEM_SPEC,
        compiler_params=pltpu.CompilerParams(vmem_limit_bytes=GRANT),
        cost_estimate=pl.CostEstimate(
            flops=4 * sums.size * H, bytes_accessed=6 * sums.size, transcendentals=0
        ),
        name="weight_partial",
    )(sums, *arrays)


def mid_kernel(partial, base, scale, con, cot, update, pre, copies):
    width = 128

    def step(k, carry):
        at = pl.ds(pl.multiple_of(k * width, width), width)
        messages = partial[0, at, :].astype(F32)
        for i in range(1, partial.shape[0]):
            messages += partial[i, at, :].astype(F32)
        preact = base[at, :] + scale[at, :] * messages
        gate = jax.nn.sigmoid(preact)
        update[at, :] = con[at, :] + preact * gate
        grad = cot[at, :] * gate * (1.0 + preact * (1.0 - gate))
        pre[at, :] = grad
        sent = (scale[at, :] * grad).astype(BF16)
        for i in range(copies.shape[0]):
            copies[i, at, :] = sent
        return carry

    lax.fori_loop(0, con.shape[0] // width, step, 0)


def mid(partial, base, scale, con, cot):
    return pl.pallas_call(
        mid_kernel,
        out_shape=(
            jax.ShapeDtypeStruct(con.shape, F32),
            jax.ShapeDtypeStruct(con.shape, F32),
            jax.ShapeDtypeStruct(partial.shape, BF16),
        ),
        in_specs=[VMEM_SPEC] * 5,
        out_specs=(VMEM_SPEC,) * 3,
        compiler_params=pltpu.CompilerParams(vmem_limit_bytes=12 << 20),
        cost_estimate=pl.CostEstimate(
            flops=24 * con.size, bytes_accessed=56 * con.size, transcendentals=con.size
        ),
        name="mid",
    )(partial, base, scale, con, cot)


def body(
    con_embed,
    var_embed,
    row_coef,
    col_coef,
    self_weight,
    msg_weight,
    timestep,
    tile_rows,
    tile_cols,
    pattern,
    cotangent,
):
    dot = functools.partial(
        jnp.dot, precision=lax.Precision.HIGHEST, preferred_element_type=F32
    )
    rows_here = con_embed.shape[0]
    z, xl, core = lax.axis_index("z"), lax.axis_index("xl"), lax.axis_index("c")
    tiles = pattern.reshape(-1, TB, TB)
    row, col = tile_rows.reshape(-1), tile_cols.reshape(-1)
    row_owner, col_owner = row // 2, col // 2
    row_at = (((row_owner % 2) ^ core) * 8 + row_owner // 2) * 2 + row % 2
    col_at = (((col_owner % 2) ^ xl) * 8 + (col_owner // 2 - z) % 8) * 2 + col % 2

    projected = (dot(var_embed, msg_weight) * col_coef[:, None]).astype(BF16)
    near = ring_gather(projected)
    far = ring_gather(swap(projected, "xl", 1))
    parts = near + [(16 + place, array) for place, array in far]
    (forward,) = tile_products(parts, col_at, row_at, hold(tiles, near[5][1]), 32, False)
    forward = forward.reshape(2, 8 * rows_here, H)
    scaled = (var_embed * col_coef[:, None]).astype(BF16)
    scaled = jnp.stack([scaled, swap(scaled, "xl", 1)])
    forward, scaled = lax.optimization_barrier((forward, scaled))
    sibling = swap(forward[1].astype(BF16), "c", 1)
    scaled, more = pair_start(scaled)
    partial = (forward[0] + sibling.astype(F32)).astype(BF16)
    partial = partial.reshape(8, rows_here, H)
    partial = lax.all_to_all(partial, ("xh", "y"), split_axis=0, concat_axis=0, tiled=True)
    frequency = jnp.exp(-math.log(10000.0) * jnp.arange(H // 2, dtype=F32) / (H // 2))
    phases = timestep[0].astype(F32) * frequency
    time_embed = jnp.concatenate([jnp.sin(phases), jnp.cos(phases)])
    base = dot(con_embed, self_weight) + time_embed[None, :]
    scale = jnp.broadcast_to(row_coef[:, None], con_embed.shape)
    partial, more, base, scale = lax.optimization_barrier((partial, more, base, scale))
    scaled = pair_end(scaled, *more)
    con_update, grad_pre, copies = mid(partial, base, scale, con_embed, cotangent)
    own = lax.all_to_all(copies, ("xh", "y"), split_axis=0, concat_axis=0, tiled=True)
    blocks = [block for _, _, block in scaled]
    own, blocks = lax.optimization_barrier((own, blocks))
    scaled = [(place, side, block) for (place, side, _), block in zip(scaled, blocks, strict=True)]
    own = own.reshape(8 * rows_here, H)
    other = swap(own, "c", 1)
    held = hold(tiles, own)
    grad_con = cotangent + dot(grad_pre, self_weight.T)
    local_self = dot(con_embed.T, grad_pre)
    backward, *first = tile_products([(0, own), (16, other)], row_at, col_at, held, 32, True)
    backward = backward.reshape(2, 8, rows_here, H)
    local_msg = weight_partial(backward, scaled)
    grad_projected, weights = scatter_and_sum(backward, first, jnp.stack([local_self, local_msg]))
    grad_lin = col_coef[:, None] * grad_projected
    grad_var = dot(grad_lin, msg_weight.T)
    return (con_update, grad_con, grad_var, weights[1], weights[0])


def solution(mesh):
    fine = Mesh(np.asarray(mesh.devices).reshape(tuple(AXES.values())), tuple(AXES))
    cg, vg = ("z", "xl"), ("xh", "y", "c")
    in_specs = (
        P(cg + vg, None),
        P(vg + cg, None),
        P(cg + vg),
        P(vg + cg),
        P(),
        P(),
        P(),
        P(cg, vg, None),
        P(cg, vg, None),
        P(cg, vg, None, None, None),
        P(cg + vg, None),
    )
    out_specs = (P(cg + vg, None), P(cg + vg, None), P(vg + cg, None), P(), P())
    return jax.shard_map(body, mesh=fine, in_specs=in_specs, out_specs=out_specs, check_vma=False)
```
